32 devices in a mesh: dom: 8 (over z, y), grp: 4 (over x, core).
Axes of the slice: x: 2, y: 2, z: 4, core: 2. Of those that a mesh axis runs over, the one named last changes fastest.
Arguments:
- profile: bfloat16 [768, 2, 64, 128], P(('dom', 'grp')), may hold values from -6 to 6
- forcing: bfloat16 [768, 2, 128], P(('dom', 'grp')), may hold values from -6 to 6
- height: bfloat16 [768, 128], P(('dom', 'grp')), may hold values from 0.5 to 2
- area: float32 [768, 128], P(('dom', 'grp')), may hold values from 0.5 to 2
- stretch: int32 [768], P(('dom', 'grp')), may hold values from 0 to 3
- face_cell: int32 [768, 128], P(('dom', 'grp')), may hold values from 0 to 127
- match_owner: int32 [8, 4, 24], P(None, 'grp'), may hold values from 0 to 7, as said below
- match_block: int32 [8, 4, 24], P(None, 'grp'), may hold values from 0 to 11
- live_blocks: int32 [32], replicated, may hold values from 6 to 24, as said below
- cell_velocity: bfloat16 [384, 2, 128], P(('dom', 'grp')), may hold values from -6 to 6
Outputs:
- wall_shear: float32 [768, 2, 128], P(('dom', 'grp'))
- wall_force: float32 [384, 2, 128], P(('dom', 'grp'))
The draws below stay inside these ranges and needn't reach their ends.
Inputs may be any that keep to these rules, and one draw needn't show every extreme that they name: `match_owner`: of the blocks of one device, at most 6 have the same owner, and in every device one owner has exactly 6. The first live_blocks blocks of a device hold faces. Among the devices of one dom index, exactly one has all 24 blocks in use.
All inputs are finite; a program needn't handle non-finite values.
Results may differ from the reference program's by a relative error of at most 0.001.
Values may be sent and summed in bfloat16 or wider, within the bound.
A program may use at most 64 MiB of HBM per device.

```python
import math
import jax
import jax.numpy as jnp
from jax import lax

NP = 64
FB = 128
BLK_DEV = 24
STEPS = 4
CBLK = 12
CAP = 6
FACEB = 768
CELLB = 384
N_DOM = 8
N_GRP = 4


def draw_match_owner(key, part):
    device_keys = jax.random.split(jax.random.fold_in(key, 7), N_DOM * N_GRP)

    def one_device(device_key):
        special_key, spread_key, place_key = jax.random.split(device_key, 3)
        special = jax.random.randint(special_key, (), 0, N_DOM, dtype=jnp.int32)
        others = jnp.arange((N_DOM - 1) * CAP, dtype=jnp.int32) // CAP
        others = others + (others >= special).astype(jnp.int32)
        picked = jax.random.permutation(spread_key, others)[:BLK_DEV - CAP]
        owner_table = jnp.concatenate([jnp.full((CAP,), special, dtype=jnp.int32), picked])
        return jax.random.permutation(place_key, owner_table)
    return jax.vmap(one_device)(device_keys).reshape(N_DOM, N_GRP, BLK_DEV).astype(jnp.int32)


def draw_live_blocks(key, part):
    base_key, full_key = jax.random.split(jax.random.fold_in(key, 11))
    counts = jax.random.randint(base_key, (N_DOM, N_GRP), BLK_DEV // 4, 7 * BLK_DEV // 8 + 1, dtype=jnp.int32)
    fullest = jax.random.randint(full_key, (N_DOM,), 0, N_GRP, dtype=jnp.int32)
    counts = jnp.where(jnp.arange(N_GRP, dtype=jnp.int32)[None, :] == fullest[:, None], BLK_DEV, counts)
    return counts.reshape(-1).astype(jnp.int32)


def set_ends(entries, own_key, least, largest):
    spot = [jax.random.randint(jax.random.fold_in(own_key, axis), (), 0, length) for axis, length in enumerate(entries.shape)]
    main_axis = entries.shape.index(max(entries.shape))
    neighbour = spot[:main_axis] + [(spot[main_axis] + 1) % entries.shape[main_axis]] + spot[main_axis + 1:]
    return entries.at[tuple(spot)].set(least).at[tuple(neighbour)].set(largest)


def level_of(own_key, shape, cuts, smallest, high):
    gain, own = 1.0, jax.random.fold_in(own_key, 6)
    for dim, blocks in cuts:
        steps = jnp.exp(jax.random.uniform(jax.random.fold_in(own, dim), (blocks,), jnp.float32, smallest / len(cuts), high / len(cuts)))
        gain = gain * jnp.repeat(steps, shape[dim] // blocks).reshape([-1 if axis == dim else 1 for axis in range(len(shape))])
    return gain


def noise(own_key, extent, scale, reach, shards=(), held_as=jnp.bfloat16):
    drawn = scale * jax.random.normal(own_key, extent, jnp.float32)
    if shards:
        drawn = drawn * level_of(own_key, extent, shards, -0.22, 0.18)
    return jnp.clip(drawn, -reach, reach).astype(held_as)


def setup_inputs(seed: int = 0) -> dict:
    key_list = jax.random.split(jax.random.key(seed), 11)
    profile = noise(key_list[0], (FACEB, 2, NP, FB), 1.0, 6.0, ((0, 32),))
    forcing = noise(key_list[1], (FACEB, 2, FB), 1.0, 6.0, ((0, 32),))
    height = jnp.clip(jnp.exp(math.log(2.0) - 1.3862944 * jax.random.uniform(key_list[2], (FACEB, FB), jnp.float32) ** level_of(key_list[2], (FACEB, FB), ((0, 32),), -0.2, 0.2)), 0.5, 2.0).astype(jnp.bfloat16)
    area = jnp.clip(jnp.exp(math.log(2.0) - 1.3862944 * jax.random.uniform(key_list[3], (FACEB, FB), jnp.float32) ** level_of(key_list[3], (FACEB, FB), ((0, 32),), -0.2, 0.2)), 0.5, 2.0)
    stretch = set_ends(jax.random.randint(key_list[4], (FACEB,), 0, 4), jax.random.fold_in(key_list[4], 1), 0, 3).astype(jnp.int32)
    face_cell = set_ends(jax.random.randint(key_list[5], (FACEB, FB), 0, FB), jax.random.fold_in(key_list[5], 1), 0, FB - 1).astype(jnp.int32)
    match_owner = draw_match_owner(jax.random.fold_in(key_list[10], 71), 0)
    match_block = set_ends(jax.random.randint(key_list[7], (N_DOM, N_GRP, BLK_DEV), 0, CBLK), jax.random.fold_in(key_list[7], 1), 0, CBLK - 1).astype(jnp.int32)
    live_blocks = draw_live_blocks(jax.random.fold_in(key_list[10], 71), 0)
    cell_velocity = noise(key_list[9], (CELLB, 2, FB), 1.0, 6.0, ((0, 32),))
    return {"profile": profile, "forcing": forcing, "height": height, "area": area, "stretch": stretch, "face_cell": face_cell, "match_owner": match_owner, "match_block": match_block, "live_blocks": live_blocks, "cell_velocity": cell_velocity}


VISCOSITY = 0.005
KARMAN = 0.41
TIME_STEP = 2.0
PUSH_GAIN = 0.5
BASE_RATE = 1.5

def wall_grid(height, stretch, points):
    levels = jnp.arange(points + 1, dtype=jnp.float32) / points
    stretch_rate = BASE_RATE + stretch.astype(jnp.float32)
    growth = jnp.exp(stretch_rate[:, None] * levels[None, :]) - 1.0
    fraction = growth / growth[:, -1:]
    depths = fraction[:, :, None] * height.astype(jnp.float32)[:, None, :]
    spacing = depths[:, 1:] - depths[:, :-1]
    middle = 0.5 * (depths[:, 1:] + depths[:, :-1])
    return (spacing, middle)

def viscosity(profile_now, spacing, middle):
    below_point = jnp.concatenate([jnp.zeros_like(profile_now[:, :, :1]), profile_now[:, :, :-1]], axis=2)
    increment = profile_now - below_point
    strain = jnp.sqrt(increment[:, 0] ** 2 + increment[:, 1] ** 2) / spacing
    return VISCOSITY + (KARMAN * middle) ** 2 * strain

def thomas_solve(lower_band, diagonal, upper_band, right_side):
    points = diagonal.shape[1]
    factor_list = []
    value_list = []
    denom = diagonal[:, 0]
    factor_now = upper_band[:, 0] / denom
    value_now = right_side[:, :, 0] / denom[:, None]
    factor_list.append(factor_now)
    value_list.append(value_now)
    for level in range(1, points):
        lower_now = lower_band[:, level]
        denom = diagonal[:, level] - lower_now * factor_now
        factor_now = upper_band[:, level] / denom
        value_now = (right_side[:, :, level] - lower_now[:, None] * value_now) / denom[:, None]
        factor_list.append(factor_now)
        value_list.append(value_now)
    answer = [None] * points
    answer[points - 1] = value_list[points - 1]
    for level in range(points - 2, -1, -1):
        answer[level] = value_list[level] - factor_list[level][:, None] * answer[level + 1]
    return jnp.stack(answer, axis=2)

def implicit_step(profile_now, source, matching, spacing, middle):
    points = spacing.shape[1]
    mixing = viscosity(profile_now, spacing, middle)
    upper_mix = jnp.concatenate([mixing[:, 1:], mixing[:, -1:]], axis=1)
    upper_gap = jnp.concatenate([spacing[:, 1:], spacing[:, -1:]], axis=1)
    centre = 0.5 * (spacing + upper_gap)
    down_coef = TIME_STEP * mixing / (spacing * centre)
    up_coef = TIME_STEP * upper_mix / (upper_gap * centre)
    row_index = lax.broadcasted_iota(jnp.int32, spacing.shape, 1)
    last_row = row_index == points - 1
    lower_band = jnp.where((row_index == 0) | last_row, 0.0, -down_coef)
    upper_band = jnp.where(last_row, 0.0, -up_coef)
    diagonal = jnp.where(last_row, 1.0, 1.0 + down_coef + up_coef)
    right_side = jnp.where(last_row[:, None], matching[:, :, None, :], profile_now + TIME_STEP * source[:, :, None, :])
    return thomas_solve(lower_band, diagonal, upper_band, right_side)

def wall_shear_of(profile_in, forcing, matching, height, stretch):
    points = profile_in.shape[2]
    spacing, middle = wall_grid(height, stretch, points)
    start_profile = profile_in.astype(jnp.float32)
    matching = matching.astype(jnp.float32)
    source = PUSH_GAIN * (forcing.astype(jnp.float32) + matching - start_profile[:, :, -1, :])
    profile_now = jnp.concatenate([start_profile[:, :, :-1], matching[:, :, None, :]], axis=2)
    for inner_step in range(STEPS):
        profile_now = implicit_step(profile_now, source, matching, spacing, middle)
    mixing = viscosity(profile_now, spacing, middle)
    return (mixing[:, 0] / spacing[:, 0])[:, None, :] * profile_now[:, :, 0]

def reference(profile, forcing, height, area, stretch, face_cell, match_owner, match_block, live_blocks, cell_velocity):
    device_total = N_DOM * N_GRP
    columns = jnp.arange(N_GRP, dtype=jnp.int32)[None, :, None]
    global_block = ((match_owner * N_GRP + columns) * CBLK + match_block).reshape(-1).astype(jnp.int32)
    slot_rows = jnp.take(cell_velocity, global_block, axis=0)
    index_grid = jnp.broadcast_to(face_cell[:, None, :], slot_rows.shape).astype(jnp.int32)
    matching = jnp.take_along_axis(slot_rows, index_grid, axis=2)
    live_mask = (jnp.arange(BLK_DEV, dtype=jnp.int32)[None, :] < live_blocks[:, None]).reshape(-1)

    def per_device(pieces):
        return wall_shear_of(pieces[0], pieces[1], pieces[2], pieces[3], pieces[4])
    shear_all = lax.map(per_device, (profile.reshape(device_total, BLK_DEV, 2, NP, FB), forcing.reshape(device_total, BLK_DEV, 2, FB), matching.reshape(device_total, BLK_DEV, 2, FB), height.reshape(device_total, BLK_DEV, FB), stretch.reshape(device_total, BLK_DEV)))
    shear_all = jnp.where(live_mask[:, None, None], shear_all.reshape(FACEB, 2, FB), 0.0)
    contrib = shear_all * area[:, None, :]
    cell_index = (global_block[:, None] * FB + face_cell).reshape(-1).astype(jnp.int32)
    face_terms = jnp.transpose(contrib, (0, 2, 1)).reshape(-1, 2)
    cell_force = jax.ops.segment_sum(face_terms, cell_index, num_segments=CELLB * FB)
    cell_force = jnp.transpose(cell_force.reshape(CELLB, FB, 2), (0, 2, 1))
    return (shear_all, cell_force)
```

```python
import functools

import jax
import jax.numpy as jnp
from jax import lax
from jax.experimental import pallas as pl
from jax.experimental.pallas import tpu as pltpu
from jax.sharding import PartitionSpec as P

STEPS = 4
VISCOSITY = 0.005
KARMAN = 0.41
TIME_STEP = 2.0
PUSH_GAIN = 0.5
BASE_RATE = 1.5
MESH = pl.DeviceIdType.MESH
F32 = jnp.float32
BF16 = jnp.bfloat16


def kernel(
    doms,
    grps,
    prof_h,
    forc_h,
    height_h,
    area_h,
    stretch_h,
    face_h,
    owner_h,
    target_h,
    live_h,
    cell_h,
    shear_ref,
    force_ref,
    prof,
    forc,
    height,
    area,
    stretch,
    face,
    owner,
    target,
    live,
    table,
    jump,
    held_f,
    held_r,
    held_t,
    base,
    quad,
    gap,
    last,
    pick,
    place,
    cells,
    packed,
    arrived,
    forc32,
    in_sem,
    own_sem,
    cell_send,
    cell_recv,
    relay_send,
    relay_recv,
    force_send,
    force_recv,
):
    blocks, _, points, faces = prof.shape
    rows = cell_h.shape[0]
    slots = doms * rows
    half = points // 2
    sub = 8
    relay = min(2, doms - 1)
    me = lax.axis_index("dom")
    mine = lax.axis_index("grp")
    wide = (blocks, faces)

    high = (2 * me) // doms
    spot = high * me + (1 - high) * (doms - 1 - me)

    def peer_at(k):
        step = k + (k - spot + doms) // doms
        return high * step + (1 - high) * (doms - 1 - step)

    barrier = pltpu.get_barrier_semaphore()
    for k in range(doms - 1):
        peer = peer_at(k)

        @pl.when((peer != 0) | (me == relay))
        def _():
            pl.semaphore_signal(barrier, inc=1, device_id={"dom": peer}, device_id_type=MESH)

    own = pltpu.make_async_copy(cell_h, table.at[me], own_sem)
    own.start()
    loads = {}
    for i, (name, src, dst) in enumerate(
        (
            ("stretch", stretch_h, stretch),
            ("height", height_h, height),
            ("owner", owner_h, owner),
            ("target", target_h, target),
            ("face", face_h, face),
            ("prof", prof_h, prof),
            ("forc", forc_h, forc),
            ("area", area_h, area),
            ("live", live_h, live),
        )
    ):
        loads[name] = pltpu.make_async_copy(src, dst, in_sem.at[i])
        loads[name].start()

    def cell_copy(slot, peer, send, recv):
        return pltpu.make_async_remote_copy(
            src_ref=table.at[slot],
            dst_ref=table.at[slot],
            send_sem=send,
            recv_sem=recv,
            device_id={"dom": peer},
            device_id_type=MESH,
        )

    def cells_of(count, send, recv):
        return pltpu.make_async_remote_copy(
            src_ref=table.at[pl.ds(0, count)],
            dst_ref=table.at[pl.ds(0, count)],
            send_sem=send,
            recv_sem=recv,
            device_id={"dom": relay},
            device_id_type=MESH,
        )

    pl.semaphore_wait(barrier, 1 + (doms - 2) * ((me + doms - 1) // doms))
    own.wait()

    @pl.when(me == 0)
    def _():
        cell_copy(0, relay, cell_send, relay_recv).start()

    @pl.when(me == relay)
    def _():
        cell_copy(0, 0, relay_send, relay_recv).wait_recv()
        for peer in range(doms - 1, 0, -1):
            if peer != relay:
                cell_copy(0, peer, relay_send, cell_recv).start()

    @pl.when(me != 0)
    def _():
        for k in range(doms - 1):
            cell_copy(me, peer_at(k), cell_send, cell_recv).start()

    eye = lax.broadcasted_iota(jnp.int32, (blocks, blocks), 0) == lax.broadcasted_iota(
        jnp.int32, (blocks, blocks), 1
    )

    def as_column(row):
        spread = jnp.broadcast_to(row.astype(F32), (blocks, blocks))
        return jnp.sum(jnp.where(eye, spread, 0.0), axis=1, keepdims=True)

    depth = sub * half
    tall_rows = sub * (half + 1)
    row_id = lax.broadcasted_iota(jnp.int32, (tall_rows, depth), 0)
    col_id = lax.broadcasted_iota(jnp.int32, (tall_rows, depth), 1)
    shift = row_id // sub - col_id % half
    same = row_id % sub == col_id // half
    turn = jnp.where(
        same, (shift == 0).astype(F32) - (shift == 1).astype(F32), 0.0
    ).astype(BF16)

    loads["stretch"].wait()
    loads["height"].wait()
    rate = BASE_RATE + as_column(stretch[...])
    tall = height[...].astype(F32)
    step_rate = jnp.broadcast_to(rate / points, wide)
    growth = jnp.exp(step_rate)
    decay = 1.0 / growth
    first = (growth - 1.0) / (jnp.exp(jnp.broadcast_to(rate, wide)) - 1.0)
    gap_scale = 0.5 * tall * first * (1.0 + growth)
    base_scale = TIME_STEP * VISCOSITY / (first * tall * gap_scale)
    quad_scale = TIME_STEP**0.5 * KARMAN / ((growth - 1.0) * gap_scale)
    mid_first = 0.5 * (1.0 + growth)

    def grid_levels(start, base_scale, quad_scale):
        chunk = min(8, half)

        def body(i, carry):
            shrink, space = carry
            for j in range(chunk):
                m = start + i * chunk + j
                base[m] = base_scale * (shrink * shrink)
                ratio = quad_scale * ((mid_first - shrink) * shrink)
                quad[m] = ratio * ratio
                gap[m] = space
                shrink = shrink * decay
                space = space * growth
            return shrink, space

        return lambda carry: lax.fori_loop(0, half // chunk, body, carry)

    shrink, space = grid_levels(0, base_scale, quad_scale)((jnp.ones(wide, F32), gap_scale))
    grid_levels(half, base_scale * growth, quad_scale * growth)((shrink, space * decay))

    for name in ("owner", "target", "face"):
        loads[name].wait()
    face_now = face[...]
    cell_ids = lax.broadcasted_iota(jnp.int32, (faces, faces), 0)
    for b in range(blocks):
        pick[b // 2, :, pl.ds(b % 2 * faces, faces)] = (
            (cell_ids == face_now[b : b + 1, :]).astype(F32).astype(BF16)
        )
    own_row = owner[me]
    aim_row = 2 * target[me]
    col_global = as_column(own_row * rows + aim_row).astype(jnp.int32)
    slot_lane = lax.broadcasted_iota(jnp.int32, (blocks, slots), 1)
    choose = jnp.concatenate(
        [(slot_lane == col_global + c).astype(F32) for c in range(2)], axis=0
    ).astype(BF16)
    terms = 4 * blocks
    widen = (
        lax.broadcasted_iota(jnp.int32, (blocks, terms), 1) // 4
        == lax.broadcasted_iota(jnp.int32, (blocks, terms), 0)
    ).astype(F32).astype(BF16)
    own_wide = jnp.dot(own_row.astype(F32).astype(BF16), widen, preferred_element_type=F32)
    aim_wide = jnp.dot(aim_row.astype(F32).astype(BF16), widen, preferred_element_type=F32)
    comp = lax.broadcasted_iota(jnp.int32, (1, terms), 1) % 2
    slot_of = (own_wide * rows + aim_wide).astype(jnp.int32) + comp
    there = (
        lax.broadcasted_iota(jnp.int32, (slots, terms), 0) == slot_of
    ).astype(F32).astype(BF16)
    place[...] = jnp.concatenate([there, there], axis=1)

    loads["prof"].wait()
    for i in range(blocks // sub):
        group = pl.ds(i * sub, sub)
        for c in range(2):
            below = None
            for part in range(2):
                levels = prof[group, c, pl.ds(part * half, half), :].reshape(depth, faces)
                steps = jnp.dot(turn, levels, preferred_element_type=F32)
                for j in range(half):
                    m = part * half + j
                    step = steps[sub * j : sub * (j + 1)]
                    if j == 0 and part:
                        step += below
                    jump[m, c, group] = gap[m, group] * step
                below = steps[depth:tall_rows]
            last[c, group] = below
    loads["forc"].wait()
    forc32[...] = forc[...].astype(F32)
    loads["area"].wait()
    loads["live"].wait()

    @pl.when(me == relay)
    def _():
        cells_of(doms - 2, cell_send, cell_recv).wait_recv()

    @pl.when(me != relay)
    def _():
        cells_of(doms - 1, cell_send, cell_recv).wait_recv()

    held = table[...].astype(F32).reshape(slots, faces).astype(BF16)
    slot_rows = jnp.dot(choose, held, preferred_element_type=F32)
    edge_low, edge_high = [], []
    for c in range(2):
        matching = jnp.take_along_axis(
            slot_rows[c * blocks : (c + 1) * blocks], face_now, axis=1, mode="promise_in_bounds"
        )
        excess = matching + last[c]
        push = forc32[pl.ds(c, blocks, stride=2), :] + excess
        source = TIME_STEP * PUSH_GAIN * push
        edge_low.append(gap[0] * source)
        edge_high.append(gap[points - 1] * source)
        jump[points - 1, c] = jump[points - 1, c] + gap[points - 1] * excess

    def speed(x):
        return 1.0 / lax.rsqrt(x[0] * x[0] + x[1] * x[1])

    def eliminate(m, ratio, carry, ends):
        x = (jump[m, 0], jump[m, 1])
        slip = 1.0 / (base[m] + quad[m] * speed(x))
        if carry is None:
            near = slip
            t = tuple(x[c] + ends[c] for c in range(2))
        else:
            above, h, t = carry
            near = slip + above
            t = tuple(x[c] + h * t[c] for c in range(2))
        f = 1.0 / (near + 1.0)
        h = ratio * f
        return slip, near, f, t, (near * h, h, t)

    def time_step(_, carry):
        low, high = None, None
        for i in range(half):
            m = i
            slip_low, near_low, f_low, t_low, low = eliminate(m, growth, low, edge_low)
            if i < half - 1:
                held_f[m] = f_low
                held_r[m] = slip_low
                for c in range(2):
                    held_t[m, c] = t_low[c]
            m = points - 1 - i
            slip_high, near_high, f_high, t_high, high = eliminate(
                m, decay, high, [-e for e in edge_high]
            )
            if i < half - 1:
                held_f[m] = f_high
                held_r[m] = slip_high
                for c in range(2):
                    held_t[m, c] = t_high[c]
        share = 1.0 / (near_low + near_high * f_high)
        down = [(t_low[c] + f_high * t_high[c]) * share for c in range(2)]
        up = [f_high * (t_high[c] + down[c]) for c in range(2)]
        for c in range(2):
            jump[half - 1, c] = slip_low * down[c]
            jump[half, c] = slip_high * up[c]
        for i in range(half - 2, -1, -1):
            for m, y in ((i, down), (points - 1 - i, up)):
                f, slip = held_f[m], held_r[m]
                for c in range(2):
                    y[c] = f * (held_t[m, c] + y[c])
                    jump[m, c] = slip * y[c]
        return carry

    lax.fori_loop(0, STEPS, time_step, 0)

    wall = (jump[0, 0], jump[0, 1])
    wall_flux = (base[0] + quad[0] * speed(wall)) * (1.0 / TIME_STEP)
    lane = lax.broadcasted_iota(jnp.int32, live.shape, 1)
    own_live = jnp.sum(
        jnp.where(lane == me * grps + mine, live[...], 0).astype(F32), axis=1, keepdims=True
    )
    alive = lax.broadcasted_iota(jnp.int32, wide, 0).astype(F32) < own_live
    size = area[...]
    for c in range(2):
        shear = jnp.where(alive, wall_flux * wall[c], 0.0)
        shear_ref[pl.ds(c, blocks, stride=2), :] = shear
        piece = shear * size
        top = piece.astype(BF16).astype(F32)
        cells[pl.ds(c, blocks, stride=4), :] = top
        cells[pl.ds(2 + c, blocks, stride=4), :] = piece - top
    upper = lax.broadcasted_iota(jnp.int32, (8, faces), 0) < 4
    for p in range(blocks // 2):
        both = cells[pl.ds(8 * p, 8), :]
        pair = jnp.concatenate(
            [jnp.where(upper, both, 0.0), jnp.where(upper, 0.0, both)], axis=1
        ).astype(BF16)
        cells[pl.ds(8 * p, 8), :] = lax.dot_general(
            pair, pick[p], (((1,), (1,)), ((), ())), preferred_element_type=F32
        )
    by_cell = cells[...]
    top = by_cell.astype(BF16)
    low = (by_cell - top.astype(F32)).astype(BF16)
    total = jnp.dot(
        place[...], jnp.concatenate([top, low], axis=0), preferred_element_type=F32
    )
    packed[...] = total.reshape(doms, rows, faces)
    for k in range(doms - 1):
        peer = peer_at(k)
        pltpu.make_async_remote_copy(
            src_ref=packed.at[peer],
            dst_ref=arrived.at[lax.rem(peer - me + doms, doms) - 1],
            send_sem=force_send,
            recv_sem=force_recv,
            device_id={"dom": peer},
            device_id_type=MESH,
        ).start()
    forces = pltpu.make_async_remote_copy(
        src_ref=packed.at[pl.ds(0, doms - 1)],
        dst_ref=arrived,
        send_sem=force_send,
        recv_sem=force_recv,
        device_id={"dom": relay},
        device_id_type=MESH,
    )
    forces.wait_recv()
    result = packed[me]
    for j in range(doms - 1):
        result += arrived[j]
    force_ref[...] = result
    forces.wait_send()

    @pl.when(me == 0)
    def _():
        cells_of(1, cell_send, relay_recv).wait_send()

    @pl.when(me != 0)
    def _():
        cells_of(doms - 1, cell_send, cell_recv).wait_send()

    @pl.when(me == relay)
    def _():
        cells_of(doms - 2, relay_send, cell_recv).wait_send()


def emit(shear_ref, force_ref, shear_out, force_out, sem):
    copies = (
        pltpu.make_async_copy(shear_ref, shear_out, sem.at[0]),
        pltpu.make_async_copy(force_ref, force_out, sem.at[1]),
    )
    for copy in copies:
        copy.start()
    for copy in copies:
        copy.wait()


def body(
    doms,
    grps,
    profile,
    forcing,
    height,
    area,
    stretch,
    face_cell,
    match_owner,
    match_block,
    live_blocks,
    cell_velocity,
):
    blocks, _, points, faces = profile.shape
    rows = 2 * cell_velocity.shape[0]
    everything = pl.BlockSpec(memory_space=pltpu.HBM)
    vmem = pl.BlockSpec(memory_space=pltpu.VMEM)
    deep = (points, blocks, faces)
    dma = pltpu.SemaphoreType.DMA
    vmem_bytes = 32 << 20
    args = (
        profile,
        forcing.reshape(2 * blocks, faces),
        height,
        area,
        stretch.reshape(1, blocks),
        face_cell,
        match_owner,
        match_block,
        live_blocks.reshape(1, -1),
        cell_velocity.reshape(rows, faces),
    )
    shear, force = pl.pallas_call(
        functools.partial(kernel, doms, grps),
        out_shape=(
            jax.ShapeDtypeStruct((2 * blocks, faces), F32),
            jax.ShapeDtypeStruct((rows, faces), F32),
        ),
        in_specs=[everything] * len(args),
        out_specs=(vmem, vmem),
        scratch_shapes=[pltpu.VMEM(arg.shape, arg.dtype) for arg in args[:-1]]
        + [
            pltpu.VMEM((doms, rows, faces), BF16),
            pltpu.VMEM((points, 2, blocks, faces), F32),
            pltpu.VMEM(deep, F32),
            pltpu.VMEM(deep, F32),
            pltpu.VMEM((points, 2, blocks, faces), F32),
            pltpu.VMEM(deep, F32),
            pltpu.VMEM(deep, F32),
            pltpu.VMEM(deep, F32),
            pltpu.VMEM((2, blocks, faces), F32),
            pltpu.VMEM((blocks // 2, faces, 2 * faces), BF16),
            pltpu.VMEM((doms * rows, 8 * blocks), BF16),
            pltpu.VMEM((4 * blocks, faces), F32),
            pltpu.VMEM((doms, rows, faces), F32),
            pltpu.VMEM((doms - 1, rows, faces), F32),
            pltpu.VMEM((2 * blocks, faces), F32),
            dma((len(args) - 1,)),
            dma,
            dma,
            dma,
            dma,
            dma,
            dma,
            dma,
        ],
        compiler_params=pltpu.CompilerParams(
            collective_id=0, has_side_effects=True, vmem_limit_bytes=vmem_bytes
        ),
        name="wall_model",
    )(*[pltpu.with_memory_space_constraint(x, pltpu.HBM) for x in args])
    shear, force = pl.pallas_call(
        emit,
        out_shape=(
            jax.ShapeDtypeStruct(shear.shape, F32),
            jax.ShapeDtypeStruct(force.shape, F32),
        ),
        in_specs=[pl.BlockSpec(memory_space=pl.ANY)] * 2,
        out_specs=(pl.BlockSpec(memory_space=pl.ANY),) * 2,
        scratch_shapes=[dma((2,))],
        compiler_params=pltpu.CompilerParams(vmem_limit_bytes=1 << 20),
        name="emit",
    )(shear, force)
    return (
        shear.reshape(blocks, 2, faces),
        force.reshape(cell_velocity.shape[0], 2, faces),
    )


def solution(mesh):
    in_specs = (
        P(("dom", "grp"), None, None, None),
        P(("dom", "grp"), None, None),
        P(("dom", "grp"), None),
        P(("dom", "grp"), None),
        P(("dom", "grp")),
        P(("dom", "grp"), None),
        P(None, "grp", None),
        P(None, "grp", None),
        P(),
        P(("dom", "grp"), None, None),
    )
    out_specs = (P(("dom", "grp"), None, None), P(("dom", "grp"), None, None))
    step = functools.partial(body, mesh.shape["dom"], mesh.shape["grp"])
    return jax.shard_map(step, mesh=mesh, in_specs=in_specs, out_specs=out_specs, check_vma=False)
```

```python
import functools

import jax
import jax.numpy as jnp
from jax import lax
from jax.experimental import pallas as pl
from jax.experimental.pallas import tpu as pltpu
from jax.sharding import PartitionSpec as P

STEPS = 4
VISCOSITY = 0.005
KARMAN = 0.41
TIME_STEP = 2.0
PUSH_GAIN = 0.5
BASE_RATE = 1.5
MESH = pl.DeviceIdType.MESH
F32 = jnp.float32
BF16 = jnp.bfloat16


def kernel(
    doms,
    grps,
    prof_h,
    forc_h,
    height_h,
    area_h,
    stretch_h,
    face_h,
    owner_h,
    target_h,
    live_h,
    cell_h,
    shear_ref,
    force_ref,
    prof,
    forc,
    height,
    area,
    stretch,
    face,
    owner,
    target,
    live,
    table,
    jump,
    held_f,
    held_r,
    held_s,
    held_t,
    fore,
    by_push,
    by_top,
    base,
    quad,
    gap,
    last,
    edge,
    pick,
    place,
    cells,
    packed,
    arrived,
    forc32,
    in_sem,
    own_sem,
    cell_send,
    cell_recv,
    relay_send,
    relay_recv,
    force_send,
    force_recv,
):
    blocks, _, points, faces = prof.shape
    rows = cell_h.shape[0]
    slots = doms * rows
    half = points // 2
    sub = 8
    relay = min(2, doms - 1)
    me = lax.axis_index("dom")
    mine = lax.axis_index("grp")
    wide = (blocks, faces)

    high = (2 * me) // doms
    spot = high * me + (1 - high) * (doms - 1 - me)

    def peer_at(k):
        step = k + (k - spot + doms) // doms
        return high * step + (1 - high) * (doms - 1 - step)

    barrier = pltpu.get_barrier_semaphore()
    for k in range(doms - 1):
        peer = peer_at(k)

        @pl.when((peer != 0) | (me == relay))
        def _():
            pl.semaphore_signal(barrier, inc=1, device_id={"dom": peer}, device_id_type=MESH)

    own = pltpu.make_async_copy(cell_h, table.at[me], own_sem)
    own.start()
    loads = {}
    for i, (name, src, dst) in enumerate(
        (
            ("stretch", stretch_h, stretch),
            ("height", height_h, height),
            ("owner", owner_h, owner),
            ("target", target_h, target),
            ("face", face_h, face),
            ("prof", prof_h, prof),
            ("forc", forc_h, forc),
            ("area", area_h, area),
            ("live", live_h, live),
        )
    ):
        loads[name] = pltpu.make_async_copy(src, dst, in_sem.at[i])
        loads[name].start()

    def cell_copy(slot, peer, send, recv):
        return pltpu.make_async_remote_copy(
            src_ref=table.at[slot],
            dst_ref=table.at[slot],
            send_sem=send,
            recv_sem=recv,
            device_id={"dom": peer},
            device_id_type=MESH,
        )

    def cells_of(count, send, recv):
        return pltpu.make_async_remote_copy(
            src_ref=table.at[pl.ds(0, count)],
            dst_ref=table.at[pl.ds(0, count)],
            send_sem=send,
            recv_sem=recv,
            device_id={"dom": relay},
            device_id_type=MESH,
        )

    pl.semaphore_wait(barrier, 1 + (doms - 2) * ((me + doms - 1) // doms))
    own.wait()

    @pl.when(me == 0)
    def _():
        cell_copy(0, relay, cell_send, relay_recv).start()

    @pl.when(me == relay)
    def _():
        cell_copy(0, 0, relay_send, relay_recv).wait_recv()
        for peer in range(doms - 1, 0, -1):
            if peer != relay:
                cell_copy(0, peer, relay_send, cell_recv).start()

    @pl.when(me != 0)
    def _():
        for k in range(doms - 1):
            cell_copy(me, peer_at(k), cell_send, cell_recv).start()

    eye = lax.broadcasted_iota(jnp.int32, (blocks, blocks), 0) == lax.broadcasted_iota(
        jnp.int32, (blocks, blocks), 1
    )

    def as_column(row):
        spread = jnp.broadcast_to(row.astype(F32), (blocks, blocks))
        return jnp.sum(jnp.where(eye, spread, 0.0), axis=1, keepdims=True)

    depth = sub * half
    tall_rows = sub * (half + 1)
    row_id = lax.broadcasted_iota(jnp.int32, (tall_rows, depth), 0)
    col_id = lax.broadcasted_iota(jnp.int32, (tall_rows, depth), 1)
    shift = row_id // sub - col_id % half
    same = row_id % sub == col_id // half
    turn = jnp.where(
        same, (shift == 0).astype(F32) - (shift == 1).astype(F32), 0.0
    ).astype(BF16)

    loads["stretch"].wait()
    loads["height"].wait()
    rate = BASE_RATE + as_column(stretch[...])
    tall = height[...].astype(F32)
    step_rate = jnp.broadcast_to(rate / points, wide)
    growth = jnp.exp(step_rate)
    decay = 1.0 / growth
    first = (growth - 1.0) / (jnp.exp(jnp.broadcast_to(rate, wide)) - 1.0)
    gap_scale = 0.5 * tall * first * (1.0 + growth)
    base_scale = TIME_STEP * VISCOSITY / (first * tall * gap_scale)
    quad_scale = TIME_STEP**0.5 * KARMAN / ((growth - 1.0) * gap_scale)
    mid_first = 0.5 * (1.0 + growth)

    def grid_levels(start, base_scale, quad_scale):
        chunk = min(8, half)

        def body(i, carry):
            shrink, space = carry
            for j in range(chunk):
                m = start + i * chunk + j
                base[m] = base_scale * (shrink * shrink)
                ratio = quad_scale * ((mid_first - shrink) * shrink)
                quad[m] = ratio * ratio
                gap[m] = space
                shrink = shrink * decay
                space = space * growth
            return shrink, space

        return lambda carry: lax.fori_loop(0, half // chunk, body, carry)

    shrink, space = grid_levels(0, base_scale, quad_scale)((jnp.ones(wide, F32), gap_scale))
    grid_levels(half, base_scale * growth, quad_scale * growth)((shrink, space * decay))

    for name in ("owner", "target", "face"):
        loads[name].wait()
    face_now = face[...]
    cell_ids = lax.broadcasted_iota(jnp.int32, (faces, faces), 0)
    for b in range(blocks):
        pick[b // 2, :, pl.ds(b % 2 * faces, faces)] = (
            (cell_ids == face_now[b : b + 1, :]).astype(F32).astype(BF16)
        )
    own_row = owner[me]
    aim_row = 2 * target[me]
    col_global = as_column(own_row * rows + aim_row).astype(jnp.int32)
    slot_lane = lax.broadcasted_iota(jnp.int32, (blocks, slots), 1)
    choose = jnp.concatenate(
        [(slot_lane == col_global + c).astype(F32) for c in range(2)], axis=0
    ).astype(BF16)
    terms = 4 * blocks
    widen = (
        lax.broadcasted_iota(jnp.int32, (blocks, terms), 1) // 4
        == lax.broadcasted_iota(jnp.int32, (blocks, terms), 0)
    ).astype(F32).astype(BF16)
    own_wide = jnp.dot(own_row.astype(F32).astype(BF16), widen, preferred_element_type=F32)
    aim_wide = jnp.dot(aim_row.astype(F32).astype(BF16), widen, preferred_element_type=F32)
    comp = lax.broadcasted_iota(jnp.int32, (1, terms), 1) % 2
    slot_of = (own_wide * rows + aim_wide).astype(jnp.int32) + comp
    there = (
        lax.broadcasted_iota(jnp.int32, (slots, terms), 0) == slot_of
    ).astype(F32).astype(BF16)
    place[...] = jnp.concatenate([there, there], axis=1)

    loads["prof"].wait()
    for i in range(blocks // sub):
        group = pl.ds(i * sub, sub)
        for c in range(2):
            below = None
            for part in range(2):
                levels = prof[group, c, pl.ds(part * half, half), :].reshape(depth, faces)
                steps = jnp.dot(turn, levels, preferred_element_type=F32)
                for j in range(half):
                    m = part * half + j
                    step = steps[sub * j : sub * (j + 1)]
                    if j == 0 and part:
                        step += below
                    jump[m, c, group] = gap[m, group] * step
                below = steps[depth:tall_rows]
            last[c, group] = below
    loads["forc"].wait()
    forc32[...] = forc[...].astype(F32)
    loads["area"].wait()
    loads["live"].wait()

    def speed(x):
        return 1.0 / lax.rsqrt(x[0] * x[0] + x[1] * x[1])

    def slip_of(m, t):
        return 1.0 / (base[m] + quad[m] * t)

    top_row = points - 1
    slip = slip_of(0, speed((jump[0, 0], jump[0, 1])))
    r = 1.0 / (slip + 1.0)
    rest = slip * r
    fore[0] = jnp.ones(wide, F32)
    held_f[0] = r
    held_r[0] = slip
    t = [jump[0, 0], jump[0, 1]]
    w = None
    for c in range(2):
        held_t[0, c] = t[c]
    for m in range(1, top_row):
        x = (jump[m, 0], jump[m, 1])
        slip = slip_of(m, speed(x))
        if m < half:
            near = slip + growth * rest
            g = growth * r
            r = 1.0 / (near + 1.0)
        else:
            near = slip + rest
            g = r
            r = 1.0 / (near + decay)
        rest = near * r
        t = [x[c] + g * t[c] for c in range(2)]
        w = g if w is None else g * w
        held_f[m] = r
        held_r[m] = slip
        fore[m] = w
        for c in range(2):
            held_t[m, c] = t[c]
    last_rest = rest
    y, push_part, top_part = None, None, None
    for m in range(top_row - 1, -1, -1):
        r, slip = held_f[m], held_r[m]
        if y is None:
            y = [r * held_t[m, c] for c in range(2)]
            push_part = r * fore[m]
            top_part = r * decay
            brink, brink_push = y, push_part
        else:
            y = [r * (held_t[m, c] + (y[c] if m < half else decay * y[c])) for c in range(2)]
            push_part = r * (fore[m] + (push_part if m < half else decay * push_part))
            top_part = r * (top_part if m < half else decay * top_part)
        for c in range(2):
            jump[m, c] = slip * y[c]
        by_push[m] = slip * push_part
        by_top[m] = slip * top_part
    edge[0] = last_rest
    edge[1] = brink_push
    for c in range(2):
        edge[2 + c] = brink[c]

    @pl.when(me == relay)
    def _():
        cells_of(doms - 2, cell_send, cell_recv).wait_recv()

    @pl.when(me != relay)
    def _():
        cells_of(doms - 1, cell_send, cell_recv).wait_recv()

    held = table[...].astype(F32).reshape(slots, faces).astype(BF16)
    slot_rows = jnp.dot(choose, held, preferred_element_type=F32)
    edge_low, edge_high, x_top = [], [], []
    for c in range(2):
        matching = jnp.take_along_axis(
            slot_rows[c * blocks : (c + 1) * blocks], face_now, axis=1, mode="promise_in_bounds"
        )
        excess = matching + last[c]
        push = forc32[pl.ds(c, blocks, stride=2), :] + excess
        source = TIME_STEP * PUSH_GAIN * push
        edge_low.append(gap[0] * source)
        edge_high.append(-gap[top_row] * source)
        x_top.append(jump[top_row, c] + gap[top_row] * excess)
    slip = slip_of(top_row, speed(x_top))
    share = 1.0 / (slip + edge[0])
    y_top = [
        (x_top[c] + edge_high[c] + edge[2 + c] + edge_low[c] * edge[1]) * share for c in range(2)
    ]
    x_top = [slip * y_top[c] for c in range(2)]

    def first_answer(m):
        if m == top_row:
            return x_top
        return [
            jump[m, c] + edge_low[c] * by_push[m] + y_top[c] * by_top[m] for c in range(2)
        ]

    def eliminate(m, ratio, state, ends, first):
        if first:
            x = first_answer(m)
            slip = slip_of(m, speed(x))
        else:
            x = [jump[m, c] for c in range(2)]
            slip = slip_of(m, held_r[m])
        if state is None:
            near = slip
            t = [x[c] + ends[c] for c in range(2)]
        else:
            above, h, t = state
            near = slip + above
            t = [x[c] + h * t[c] for c in range(2)]
        f = 1.0 / (near + 1.0)
        h = ratio * f
        return slip, near, f, t, (near * h, h, t)

    def forward(first):
        low, high = None, None
        for i in range(half):
            for m in (i, top_row - i):
                if m == i:
                    slip, near, f, t, low = ends_low = eliminate(m, growth, low, edge_low, first)
                else:
                    slip, near, f, t, high = ends_high = eliminate(m, decay, high, edge_high, first)
                if i < half - 1:
                    held_f[m] = f
                    held_s[m] = slip
                    for c in range(2):
                        held_t[m, c] = t[c]
        return ends_low, ends_high

    def settle(m, slip, y):
        x = [slip * y[c] for c in range(2)]
        for c in range(2):
            jump[m, c] = x[c]
        held_r[m] = speed(x)

    def backward(ends_low, ends_high, final):
        slip_low, near_low, _, t_low, _ = ends_low
        slip_high, near_high, f_high, t_high, _ = ends_high
        share = 1.0 / (near_low + near_high * f_high)
        down = [(t_low[c] + f_high * t_high[c]) * share for c in range(2)]
        up = [f_high * (t_high[c] + down[c]) for c in range(2)]
        if not final:
            settle(half - 1, slip_low, down)
            settle(half, slip_high, up)
        for i in range(half - 2, -1, -1):
            for m, y in ((i, down), (top_row - i, up)):
                if final and m != i:
                    continue
                f = held_f[m]
                for c in range(2):
                    y[c] = f * (held_t[m, c] + y[c])
                if not final:
                    settle(m, held_s[m], y)
        return down

    for step in range(1, STEPS):
        ends = forward(step == 1)
        down = backward(*ends, step == STEPS - 1)

    wall = [held_s[0] * down[c] for c in range(2)]
    wall_flux = (base[0] + quad[0] * speed(wall)) * (1.0 / TIME_STEP)
    lane = lax.broadcasted_iota(jnp.int32, live.shape, 1)
    own_live = jnp.sum(
        jnp.where(lane == me * grps + mine, live[...], 0).astype(F32), axis=1, keepdims=True
    )
    alive = lax.broadcasted_iota(jnp.int32, wide, 0).astype(F32) < own_live
    size = area[...]
    for c in range(2):
        shear = jnp.where(alive, wall_flux * wall[c], 0.0)
        shear_ref[pl.ds(c, blocks, stride=2), :] = shear
        piece = shear * size
        top = piece.astype(BF16).astype(F32)
        cells[pl.ds(c, blocks, stride=4), :] = top
        cells[pl.ds(2 + c, blocks, stride=4), :] = piece - top
    upper = lax.broadcasted_iota(jnp.int32, (8, faces), 0) < 4
    for p in range(blocks // 2):
        both = cells[pl.ds(8 * p, 8), :]
        pair = jnp.concatenate(
            [jnp.where(upper, both, 0.0), jnp.where(upper, 0.0, both)], axis=1
        ).astype(BF16)
        cells[pl.ds(8 * p, 8), :] = lax.dot_general(
            pair, pick[p], (((1,), (1,)), ((), ())), preferred_element_type=F32
        )
    by_cell = cells[...]
    top = by_cell.astype(BF16)
    low = (by_cell - top.astype(F32)).astype(BF16)
    total = jnp.dot(
        place[...], jnp.concatenate([top, low], axis=0), preferred_element_type=F32
    )
    packed[...] = total.reshape(doms, rows, faces)
    for k in range(doms - 1):
        peer = peer_at(k)
        pltpu.make_async_remote_copy(
            src_ref=packed.at[peer],
            dst_ref=arrived.at[lax.rem(peer - me + doms, doms) - 1],
            send_sem=force_send,
            recv_sem=force_recv,
            device_id={"dom": peer},
            device_id_type=MESH,
        ).start()
    forces = pltpu.make_async_remote_copy(
        src_ref=packed.at[pl.ds(0, doms - 1)],
        dst_ref=arrived,
        send_sem=force_send,
        recv_sem=force_recv,
        device_id={"dom": relay},
        device_id_type=MESH,
    )
    forces.wait_recv()
    result = packed[me]
    for j in range(doms - 1):
        result += arrived[j]
    force_ref[...] = result
    forces.wait_send()

    @pl.when(me == 0)
    def _():
        cells_of(1, cell_send, relay_recv).wait_send()

    @pl.when(me != 0)
    def _():
        cells_of(doms - 1, cell_send, cell_recv).wait_send()

    @pl.when(me == relay)
    def _():
        cells_of(doms - 2, relay_send, cell_recv).wait_send()


def emit(shear_ref, force_ref, shear_out, force_out, sem):
    copies = (
        pltpu.make_async_copy(shear_ref, shear_out, sem.at[0]),
        pltpu.make_async_copy(force_ref, force_out, sem.at[1]),
    )
    for copy in copies:
        copy.start()
    for copy in copies:
        copy.wait()


def body(
    doms,
    grps,
    profile,
    forcing,
    height,
    area,
    stretch,
    face_cell,
    match_owner,
    match_block,
    live_blocks,
    cell_velocity,
):
    blocks, _, points, faces = profile.shape
    rows = 2 * cell_velocity.shape[0]
    everything = pl.BlockSpec(memory_space=pltpu.HBM)
    vmem = pl.BlockSpec(memory_space=pltpu.VMEM)
    deep = (points, blocks, faces)
    dma = pltpu.SemaphoreType.DMA
    vmem_bytes = 32 << 20
    args = (
        profile,
        forcing.reshape(2 * blocks, faces),
        height,
        area,
        stretch.reshape(1, blocks),
        face_cell,
        match_owner,
        match_block,
        live_blocks.reshape(1, -1),
        cell_velocity.reshape(rows, faces),
    )
    shear, force = pl.pallas_call(
        functools.partial(kernel, doms, grps),
        out_shape=(
            jax.ShapeDtypeStruct((2 * blocks, faces), F32),
            jax.ShapeDtypeStruct((rows, faces), F32),
        ),
        in_specs=[everything] * len(args),
        out_specs=(vmem, vmem),
        scratch_shapes=[pltpu.VMEM(arg.shape, arg.dtype) for arg in args[:-1]]
        + [
            pltpu.VMEM((doms, rows, faces), BF16),
            pltpu.VMEM((points, 2, blocks, faces), F32),
            pltpu.VMEM(deep, F32),
            pltpu.VMEM(deep, F32),
            pltpu.VMEM(deep, F32),
            pltpu.VMEM((points, 2, blocks, faces), F32),
            pltpu.VMEM(deep, F32),
            pltpu.VMEM(deep, F32),
            pltpu.VMEM(deep, F32),
            pltpu.VMEM(deep, F32),
            pltpu.VMEM(deep, F32),
            pltpu.VMEM(deep, F32),
            pltpu.VMEM((2, blocks, faces), F32),
            pltpu.VMEM((4, blocks, faces), F32),
            pltpu.VMEM((blocks // 2, faces, 2 * faces), BF16),
            pltpu.VMEM((doms * rows, 8 * blocks), BF16),
            pltpu.VMEM((4 * blocks, faces), F32),
            pltpu.VMEM((doms, rows, faces), F32),
            pltpu.VMEM((doms - 1, rows, faces), F32),
            pltpu.VMEM((2 * blocks, faces), F32),
            dma((len(args) - 1,)),
            dma,
            dma,
            dma,
            dma,
            dma,
            dma,
            dma,
        ],
        compiler_params=pltpu.CompilerParams(
            collective_id=0, has_side_effects=True, vmem_limit_bytes=vmem_bytes
        ),
        name="wall_model",
    )(*[pltpu.with_memory_space_constraint(x, pltpu.HBM) for x in args])
    shear, force = pl.pallas_call(
        emit,
        out_shape=(
            jax.ShapeDtypeStruct(shear.shape, F32),
            jax.ShapeDtypeStruct(force.shape, F32),
        ),
        in_specs=[pl.BlockSpec(memory_space=pl.ANY)] * 2,
        out_specs=(pl.BlockSpec(memory_space=pl.ANY),) * 2,
        scratch_shapes=[dma((2,))],
        compiler_params=pltpu.CompilerParams(vmem_limit_bytes=1 << 20),
        name="emit",
    )(shear, force)
    return (
        shear.reshape(blocks, 2, faces),
        force.reshape(cell_velocity.shape[0], 2, faces),
    )


def solution(mesh):
    in_specs = (
        P(("dom", "grp"), None, None, None),
        P(("dom", "grp"), None, None),
        P(("dom", "grp"), None),
        P(("dom", "grp"), None),
        P(("dom", "grp")),
        P(("dom", "grp"), None),
        P(None, "grp", None),
        P(None, "grp", None),
        P(),
        P(("dom", "grp"), None, None),
    )
    out_specs = (P(("dom", "grp"), None, None), P(("dom", "grp"), None, None))
    step = functools.partial(body, mesh.shape["dom"], mesh.shape["grp"])
    return jax.shard_map(step, mesh=mesh, in_specs=in_specs, out_specs=out_specs, check_vma=False)
```

```python
import functools

import jax
import jax.numpy as jnp
from jax import lax
from jax.experimental import pallas as pl
from jax.experimental.pallas import tpu as pltpu
from jax.sharding import PartitionSpec as P

STEPS = 4
VISCOSITY = 0.005
KARMAN = 0.41
TIME_STEP = 2.0
PUSH_GAIN = 0.5
BASE_RATE = 1.5
MESH = pl.DeviceIdType.MESH
F32 = jnp.float32
BF16 = jnp.bfloat16


def kernel(
    doms,
    grps,
    prof_h,
    forc_h,
    height_h,
    area_h,
    stretch_h,
    face_h,
    owner_h,
    target_h,
    live_h,
    cell_h,
    shear_ref,
    force_ref,
    prof,
    forc,
    height,
    area,
    stretch,
    face,
    owner,
    target,
    live,
    table,
    jump,
    held_f,
    held_r,
    held_s,
    held_t,
    fore,
    by_push,
    by_top,
    base,
    quad,
    gap,
    last,
    edge,
    middle,
    held,
    rows_of,
    owner_s,
    target_s,
    row_at,
    pick,
    place,
    cells,
    packed,
    arrived,
    forc32,
    in_sem,
    own_sem,
    cell_send,
    cell_recv,
    relay_send,
    relay_recv,
    force_send,
    force_recv,
):
    blocks, _, points, faces = prof.shape
    rows = cell_h.shape[0]
    slots = doms * rows
    half = points // 2
    sub = 8
    relay = min(2, doms - 1)
    me = lax.axis_index("dom")
    mine = lax.axis_index("grp")
    wide = (blocks, faces)

    high = (2 * me) // doms
    odd = (1 - high) * (me % 2) if doms % 2 == 0 else 0
    spot = high * me + (1 - high) * (doms - 1 - me + odd)

    def peer_at(k):
        step = k + (k - spot + doms) // doms
        peer = high * step + (1 - high) * (doms - 1 - step)
        return peer + odd * (1 - 2 * (peer % 2))

    barrier = pltpu.get_barrier_semaphore()
    first = doms // 2 - 1
    for j in list(range(first, doms)) + list(range(1, first)):
        peer = lax.rem(me + j, doms)

        @pl.when((peer != 0) | (me == relay))
        def _():
            pl.semaphore_signal(barrier, inc=1, device_id={"dom": peer}, device_id_type=MESH)

    own = pltpu.make_async_copy(cell_h, table.at[me], own_sem)
    own.start()
    loads = {}
    for i, (name, src, dst) in enumerate(
        (
            ("stretch", stretch_h, stretch),
            ("height", height_h, height),
            ("owner", owner_h, owner),
            ("target", target_h, target),
            ("face", face_h, face),
            ("prof", prof_h, prof),
            ("forc", forc_h, forc),
            ("area", area_h, area),
            ("live", live_h, live),
            ("owner_s", owner_h.at[me], owner_s),
            ("target_s", target_h.at[me], target_s),
        )
    ):
        loads[name] = pltpu.make_async_copy(src, dst, in_sem.at[i])
        loads[name].start()

    peers = [peer_at(k) for k in range(doms - 1)]

    def cell_copy(slot, peer, send, recv):
        return pltpu.make_async_remote_copy(
            src_ref=table.at[slot],
            dst_ref=table.at[slot],
            send_sem=send,
            recv_sem=recv,
            device_id={"dom": peer},
            device_id_type=MESH,
        )

    def cells_of(count, send, recv):
        return pltpu.make_async_remote_copy(
            src_ref=table.at[pl.ds(0, count)],
            dst_ref=table.at[pl.ds(0, count)],
            send_sem=send,
            recv_sem=recv,
            device_id={"dom": relay},
            device_id_type=MESH,
        )

    pl.semaphore_wait(barrier, 1 + (doms - 2) * ((me + doms - 1) // doms))
    own.wait()

    @pl.when(me == 0)
    def _():
        cell_copy(0, relay, cell_send, relay_recv).start()

    @pl.when(me == relay)
    def _():
        cell_copy(0, 1, relay_send, relay_recv).wait_recv()

    @pl.when(me != 0)
    def _():
        for peer in peers:

            @pl.when((me == relay) & (peer != 0))
            def _():
                cell_copy(0, peer, relay_send, cell_recv).start()

            cell_copy(me, peer, cell_send, cell_recv).start()

    eye = lax.broadcasted_iota(jnp.int32, (blocks, blocks), 0) == lax.broadcasted_iota(
        jnp.int32, (blocks, blocks), 1
    )

    def as_column(row):
        spread = jnp.broadcast_to(row.astype(F32), (blocks, blocks))
        return jnp.sum(jnp.where(eye, spread, 0.0), axis=1, keepdims=True)

    depth = sub * half
    tall_rows = sub * (half + 1)
    row_id = lax.broadcasted_iota(jnp.int32, (tall_rows, depth), 0)
    col_id = lax.broadcasted_iota(jnp.int32, (tall_rows, depth), 1)
    shift = row_id // sub - col_id % half
    same = row_id % sub == col_id // half
    turn = jnp.where(
        same, (shift == 0).astype(F32) - (shift == 1).astype(F32), 0.0
    ).astype(BF16)

    loads["stretch"].wait()
    loads["height"].wait()
    rate = BASE_RATE + as_column(stretch[...])
    tall = height[...].astype(F32)
    step_rate = jnp.broadcast_to(rate / points, wide)
    growth = jnp.exp(step_rate)
    decay = 1.0 / growth
    first = (growth - 1.0) / (jnp.exp(jnp.broadcast_to(rate, wide)) - 1.0)
    gap_scale = 0.5 * tall * first * (1.0 + growth)
    base_scale = TIME_STEP * VISCOSITY / (first * tall * gap_scale)
    quad_scale = TIME_STEP**0.5 * KARMAN / ((growth - 1.0) * gap_scale)
    mid_first = 0.5 * (1.0 + growth)

    def grid_levels(start, base_scale, quad_scale):
        chunk = min(8, half)

        def body(i, carry):
            shrink, space = carry
            for j in range(chunk):
                m = start + i * chunk + j
                base[m] = base_scale * (shrink * shrink)
                ratio = quad_scale * ((mid_first - shrink) * shrink)
                quad[m] = ratio * ratio
                gap[m] = space
                shrink = shrink * decay
                space = space * growth
            return shrink, space

        return lambda carry: lax.fori_loop(0, half // chunk, body, carry)

    shrink, space = grid_levels(0, base_scale, quad_scale)((jnp.ones(wide, F32), gap_scale))
    grid_levels(half, base_scale * growth, quad_scale * growth)((shrink, space * decay))

    for name in ("owner", "target", "face"):
        loads[name].wait()
    face_now = face[...]
    face_down = jnp.transpose(face_now.astype(F32))
    cell_ids = lax.broadcasted_iota(jnp.int32, (faces, faces), 1).astype(F32)
    for b in range(blocks):
        pick[b // 2, pl.ds(b % 2 * faces, faces), :] = (
            (cell_ids == face_down[:, b : b + 1]).astype(F32).astype(BF16)
        )
    own_row = owner[me]
    aim_row = 2 * target[me]
    terms = 4 * blocks
    widen = (
        lax.broadcasted_iota(jnp.int32, (blocks, terms), 1) // 4
        == lax.broadcasted_iota(jnp.int32, (blocks, terms), 0)
    ).astype(F32).astype(BF16)
    own_wide = jnp.dot(own_row.astype(F32).astype(BF16), widen, preferred_element_type=F32)
    aim_wide = jnp.dot(aim_row.astype(F32).astype(BF16), widen, preferred_element_type=F32)
    comp = lax.broadcasted_iota(jnp.int32, (1, terms), 1) % 2
    slot_of = (own_wide * rows + aim_wide).astype(jnp.int32) + comp
    there = (
        lax.broadcasted_iota(jnp.int32, (slots, terms), 0) == slot_of
    ).astype(F32).astype(BF16)
    place[...] = jnp.concatenate([there, there], axis=1)

    loads["prof"].wait()
    for i in range(blocks // sub):
        group = pl.ds(i * sub, sub)
        for c in range(2):
            below = None
            for part in range(2):
                levels = prof[group, c, pl.ds(part * half, half), :].reshape(depth, faces)
                steps = jnp.dot(turn, levels, preferred_element_type=F32)
                for j in range(half):
                    m = part * half + j
                    step = steps[sub * j : sub * (j + 1)]
                    if j == 0 and part:
                        step += below
                    jump[m, c, group] = gap[m, group] * step
                below = steps[depth:tall_rows]
            last[c, group] = below
    for name in ("owner_s", "target_s"):
        loads[name].wait()
    for b in range(blocks):
        row_at[b] = owner_s[0, b] * rows + 2 * target_s[0, b]
    loads["forc"].wait()
    forc32[...] = forc[...].astype(F32)
    loads["area"].wait()
    loads["live"].wait()

    def speed(x):
        return 1.0 / lax.rsqrt(x[0] * x[0] + x[1] * x[1])

    def slip_of(m, t):
        return 1.0 / (base[m] + quad[m] * t)

    top_row = points - 1
    slip = slip_of(0, speed((jump[0, 0], jump[0, 1])))
    r = 1.0 / (slip + 1.0)
    rest = slip * r
    fore[0] = jnp.ones(wide, F32)
    held_f[0] = r
    held_r[0] = slip
    t = [jump[0, 0], jump[0, 1]]
    w = None
    for c in range(2):
        held_t[0, c] = t[c]
    for m in range(1, top_row):
        x = (jump[m, 0], jump[m, 1])
        slip = slip_of(m, speed(x))
        if m < half:
            near = slip + growth * rest
            g = growth * r
            r = 1.0 / (near + 1.0)
        else:
            near = slip + rest
            g = r
            r = 1.0 / (near + decay)
        rest = near * r
        t = [x[c] + g * t[c] for c in range(2)]
        w = g if w is None else g * w
        held_f[m] = r
        held_r[m] = slip
        fore[m] = w
        for c in range(2):
            held_t[m, c] = t[c]
    last_rest = rest
    y, push_part, top_part = None, None, None
    for m in range(top_row - 1, -1, -1):
        r, slip = held_f[m], held_r[m]
        if y is None:
            y = [r * held_t[m, c] for c in range(2)]
            push_part = r * fore[m]
            top_part = r * decay
            brink, brink_push = y, push_part
        else:
            y = [r * (held_t[m, c] + (y[c] if m < half else decay * y[c])) for c in range(2)]
            push_part = r * (fore[m] + (push_part if m < half else decay * push_part))
            top_part = r * (top_part if m < half else decay * top_part)
        for c in range(2):
            jump[m, c] = slip * y[c]
        by_push[m] = slip * push_part
        by_top[m] = slip * top_part
    edge[0] = last_rest
    edge[1] = brink_push
    for c in range(2):
        edge[2 + c] = brink[c]

    @pl.when(me == relay)
    def _():
        cells_of(doms - 2, cell_send, cell_recv).wait_recv()

    @pl.when(me != relay)
    def _():
        cells_of(doms - 1, cell_send, cell_recv).wait_recv()

    held[...] = table[...].astype(F32).reshape(slots, faces)
    for b in range(blocks):
        rows_of[pl.ds(2 * b, 2), :] = held[pl.ds(row_at[b], 2), :]
    edge_low, edge_high, x_top = [], [], []
    for c in range(2):
        matching = jnp.take_along_axis(
            rows_of[pl.ds(c, blocks, stride=2), :], face_now, axis=1, mode="promise_in_bounds"
        )
        excess = matching + last[c]
        push = forc32[pl.ds(c, blocks, stride=2), :] + excess
        source = TIME_STEP * PUSH_GAIN * push
        edge_low.append(gap[0] * source)
        edge_high.append(-gap[top_row] * source)
        x_top.append(jump[top_row, c] + gap[top_row] * excess)
    slip = slip_of(top_row, speed(x_top))
    share = 1.0 / (slip + edge[0])
    y_top = [
        (x_top[c] + edge_high[c] + edge[2 + c] + edge_low[c] * edge[1]) * share for c in range(2)
    ]
    x_top = [slip * y_top[c] for c in range(2)]

    def first_answer(m):
        if m == top_row:
            return x_top
        return [
            jump[m, c] + edge_low[c] * by_push[m] + y_top[c] * by_top[m] for c in range(2)
        ]

    def eliminate(m, ratio, state, ends, first):
        if first:
            x = first_answer(m)
            slip = slip_of(m, speed(x))
        else:
            x = [jump[m, c] for c in range(2)]
            slip = slip_of(m, held_r[m])
        if state is None:
            near = slip
            t = [x[c] + ends[c] for c in range(2)]
        else:
            above, h, t = state
            near = slip + above
            t = [x[c] + h * t[c] for c in range(2)]
        f = 1.0 / (near + 1.0)
        h = ratio * f
        return slip, near, f, t, (near * h, h, t)

    def forward(first):
        low, high = None, None
        for i in range(half):
            for m in (i, top_row - i):
                if m == i:
                    slip, near, f, t, low = eliminate(m, growth, low, edge_low, first)
                else:
                    slip, near, f, t, high = eliminate(m, decay, high, edge_high, first)
                held_f[m] = f
                held_s[m] = slip
                for c in range(2):
                    held_t[m, c] = t[c]
                if i == half - 1:
                    middle[m - i] = near

    def settle(m, y):
        slip = held_s[m]
        x = [slip * y[c] for c in range(2)]
        for c in range(2):
            jump[m, c] = x[c]
        held_r[m] = speed(x)

    def backward(final):
        f_high = held_f[half]
        share = 1.0 / (middle[0] + middle[1] * f_high)
        down, up = [], []
        for c in range(2):
            t_high = held_t[half, c]
            down.append((held_t[half - 1, c] + f_high * t_high) * share)
            up.append(f_high * (t_high + down[c]))
        if not final:
            settle(half - 1, down)
            settle(half, up)
        for i in range(half - 2, -1, -1):
            for m, y in ((i, down), (top_row - i, up)):
                if final and m != i:
                    continue
                f = held_f[m]
                for c in range(2):
                    y[c] = f * (held_t[m, c] + y[c])
                if not final:
                    settle(m, y)
        return down

    forward(True)

    def time_step(_, carry):
        backward(False)
        forward(False)
        return carry

    lax.fori_loop(2, STEPS, time_step, 0)
    down = backward(True)

    wall = [held_s[0] * down[c] for c in range(2)]
    wall_flux = (base[0] + quad[0] * speed(wall)) * (1.0 / TIME_STEP)
    lane = lax.broadcasted_iota(jnp.int32, live.shape, 1)
    own_live = jnp.sum(
        jnp.where(lane == me * grps + mine, live[...], 0).astype(F32), axis=1, keepdims=True
    )
    alive = lax.broadcasted_iota(jnp.int32, wide, 0).astype(F32) < own_live
    size = area[...]
    for c in range(2):
        shear = jnp.where(alive, wall_flux * wall[c], 0.0)
        shear_ref[pl.ds(c, blocks, stride=2), :] = shear
        piece = shear * size
        top = piece.astype(BF16).astype(F32)
        cells[pl.ds(c, blocks, stride=4), :] = top
        cells[pl.ds(2 + c, blocks, stride=4), :] = piece - top
    upper = lax.broadcasted_iota(jnp.int32, (8, faces), 0) < 4
    for p in range(blocks // 2):
        both = cells[pl.ds(8 * p, 8), :]
        pair = jnp.concatenate(
            [jnp.where(upper, both, 0.0), jnp.where(upper, 0.0, both)], axis=1
        ).astype(BF16)
        cells[pl.ds(8 * p, 8), :] = jnp.dot(pair, pick[p], preferred_element_type=F32)
    by_cell = cells[...]
    top = by_cell.astype(BF16)
    low = (by_cell - top.astype(F32)).astype(BF16)
    total = jnp.dot(
        place[...], jnp.concatenate([top, low], axis=0), preferred_element_type=F32
    )
    packed[...] = total.reshape(doms, rows, faces)
    for peer in peers:
        pltpu.make_async_remote_copy(
            src_ref=packed.at[peer],
            dst_ref=arrived.at[lax.rem(peer - me + doms, doms) - 1],
            send_sem=force_send,
            recv_sem=force_recv,
            device_id={"dom": peer},
            device_id_type=MESH,
        ).start()
    forces = pltpu.make_async_remote_copy(
        src_ref=packed.at[pl.ds(0, doms - 1)],
        dst_ref=arrived,
        send_sem=force_send,
        recv_sem=force_recv,
        device_id={"dom": relay},
        device_id_type=MESH,
    )
    forces.wait_recv()
    result = packed[me]
    for j in range(doms - 1):
        result += arrived[j]
    force_ref[...] = result
    forces.wait_send()

    @pl.when(me == 0)
    def _():
        cells_of(1, cell_send, relay_recv).wait_send()

    @pl.when(me != 0)
    def _():
        cells_of(doms - 1, cell_send, cell_recv).wait_send()

    @pl.when(me == relay)
    def _():
        cells_of(doms - 2, relay_send, cell_recv).wait_send()


def emit(shear_ref, force_ref, shear_out, force_out, sem):
    copies = (
        pltpu.make_async_copy(shear_ref, shear_out, sem.at[0]),
        pltpu.make_async_copy(force_ref, force_out, sem.at[1]),
    )
    for copy in copies:
        copy.start()
    for copy in copies:
        copy.wait()


def body(
    doms,
    grps,
    profile,
    forcing,
    height,
    area,
    stretch,
    face_cell,
    match_owner,
    match_block,
    live_blocks,
    cell_velocity,
):
    blocks, _, points, faces = profile.shape
    rows = 2 * cell_velocity.shape[0]
    everything = pl.BlockSpec(memory_space=pltpu.HBM)
    vmem = pl.BlockSpec(memory_space=pltpu.VMEM)
    deep = (points, blocks, faces)
    dma = pltpu.SemaphoreType.DMA
    vmem_bytes = 32 << 20
    args = (
        profile,
        forcing.reshape(2 * blocks, faces),
        height,
        area,
        stretch.reshape(1, blocks),
        face_cell,
        match_owner,
        match_block,
        live_blocks.reshape(1, -1),
        cell_velocity.reshape(rows, faces),
    )
    shear, force = pl.pallas_call(
        functools.partial(kernel, doms, grps),
        out_shape=(
            jax.ShapeDtypeStruct((2 * blocks, faces), F32),
            jax.ShapeDtypeStruct((rows, faces), F32),
        ),
        in_specs=[everything] * len(args),
        out_specs=(vmem, vmem),
        scratch_shapes=[pltpu.VMEM(arg.shape, arg.dtype) for arg in args[:-1]]
        + [
            pltpu.VMEM((doms, rows, faces), BF16),
            pltpu.VMEM((points, 2, blocks, faces), F32),
            pltpu.VMEM(deep, F32),
            pltpu.VMEM(deep, F32),
            pltpu.VMEM(deep, F32),
            pltpu.VMEM((points, 2, blocks, faces), F32),
            pltpu.VMEM(deep, F32),
            pltpu.VMEM(deep, F32),
            pltpu.VMEM(deep, F32),
            pltpu.VMEM(deep, F32),
            pltpu.VMEM(deep, F32),
            pltpu.VMEM(deep, F32),
            pltpu.VMEM((2, blocks, faces), F32),
            pltpu.VMEM((4, blocks, faces), F32),
            pltpu.VMEM((2, blocks, faces), F32),
            pltpu.VMEM((doms * rows, faces), F32),
            pltpu.VMEM((2 * blocks, faces), F32),
            pltpu.SMEM((1, blocks), jnp.int32),
            pltpu.SMEM((1, blocks), jnp.int32),
            pltpu.SMEM((blocks,), jnp.int32),
            pltpu.VMEM((blocks // 2, 2 * faces, faces), BF16),
            pltpu.VMEM((doms * rows, 8 * blocks), BF16),
            pltpu.VMEM((4 * blocks, faces), F32),
            pltpu.VMEM((doms, rows, faces), F32),
            pltpu.VMEM((doms - 1, rows, faces), F32),
            pltpu.VMEM((2 * blocks, faces), F32),
            dma((len(args) + 1,)),
            dma,
            dma,
            dma,
            dma,
            dma,
            dma,
            dma,
        ],
        compiler_params=pltpu.CompilerParams(
            collective_id=0, has_side_effects=True, vmem_limit_bytes=vmem_bytes
        ),
        name="wall_model",
    )(*[pltpu.with_memory_space_constraint(x, pltpu.HBM) for x in args])
    shear, force = pl.pallas_call(
        emit,
        out_shape=(
            jax.ShapeDtypeStruct(shear.shape, F32),
            jax.ShapeDtypeStruct(force.shape, F32),
        ),
        in_specs=[pl.BlockSpec(memory_space=pl.ANY)] * 2,
        out_specs=(pl.BlockSpec(memory_space=pl.ANY),) * 2,
        scratch_shapes=[dma((2,))],
        compiler_params=pltpu.CompilerParams(vmem_limit_bytes=1 << 20),
        name="emit",
    )(shear, force)
    return (
        shear.reshape(blocks, 2, faces),
        force.reshape(cell_velocity.shape[0], 2, faces),
    )


def solution(mesh):
    in_specs = (
        P(("dom", "grp"), None, None, None),
        P(("dom", "grp"), None, None),
        P(("dom", "grp"), None),
        P(("dom", "grp"), None),
        P(("dom", "grp")),
        P(("dom", "grp"), None),
        P(None, "grp", None),
        P(None, "grp", None),
        P(),
        P(("dom", "grp"), None, None),
    )
    out_specs = (P(("dom", "grp"), None, None), P(("dom", "grp"), None, None))
    step = functools.partial(body, mesh.shape["dom"], mesh.shape["grp"])
    return jax.shard_map(step, mesh=mesh, in_specs=in_specs, out_specs=out_specs, check_vma=False)
```

```python
import functools

import jax
import jax.numpy as jnp
from jax import lax
from jax.experimental import pallas as pl
from jax.experimental.pallas import tpu as pltpu
from jax.sharding import PartitionSpec as P

STEPS = 4
VISCOSITY = 0.005
KARMAN = 0.41
TIME_STEP = 2.0
PUSH_GAIN = 0.5
BASE_RATE = 1.5
MESH = pl.DeviceIdType.MESH
F32 = jnp.float32
BF16 = jnp.bfloat16


def kernel(
    doms,
    grps,
    prof_h,
    forc_h,
    height_h,
    area_h,
    stretch_h,
    face_h,
    owner_h,
    target_h,
    live_h,
    cell_h,
    shear_ref,
    force_ref,
    prof,
    forc,
    height,
    area,
    stretch,
    face,
    owner,
    target,
    live,
    table,
    jump,
    held_f,
    held_r,
    held_s,
    held_t,
    fore,
    by_push,
    by_top,
    base,
    quad,
    gap,
    last,
    edge,
    middle,
    scale,
    held,
    rows_of,
    owner_s,
    target_s,
    row_at,
    spot_at,
    early_out,
    pick,
    place,
    cells,
    packed,
    arrived,
    forc32,
    cell_send,
    cell_recv,
    relay_send,
    relay_recv,
    force_send,
    force_recv,
):
    blocks, _, points, faces = prof.shape
    rows = cell_h.shape[0]
    slots = doms * rows
    half = points // 2
    sub = 8
    relay = min(2, doms - 1)
    me = lax.axis_index("dom")
    mine = lax.axis_index("grp")
    wide = (blocks, faces)

    high = (2 * me) // doms
    odd = (1 - high) * (me % 2) if doms % 2 == 0 else 0
    spot = high * me + (1 - high) * (doms - 1 - me + odd)

    def peer_at(k):
        step = k + (k - spot + doms) // doms
        peer = high * step + (1 - high) * (doms - 1 - step)
        return peer + odd * (1 - 2 * (peer % 2))

    barrier = pltpu.get_barrier_semaphore()
    first = doms // 2 - 1
    for j in list(range(first, doms)) + list(range(1, first)):
        peer = lax.rem(me + j, doms)

        @pl.when((peer != 0) | (me == relay))
        def _():
            pl.semaphore_signal(barrier, inc=1, device_id={"dom": peer}, device_id_type=MESH)

    peers = [peer_at(k) for k in range(doms - 1)]

    def cell_copy(slot, peer, send, recv):
        return pltpu.make_async_remote_copy(
            src_ref=table.at[slot],
            dst_ref=table.at[slot],
            send_sem=send,
            recv_sem=recv,
            device_id={"dom": peer},
            device_id_type=MESH,
        )

    def cells_of(count, send, recv):
        return pltpu.make_async_remote_copy(
            src_ref=table.at[pl.ds(0, count)],
            dst_ref=table.at[pl.ds(0, count)],
            send_sem=send,
            recv_sem=recv,
            device_id={"dom": relay},
            device_id_type=MESH,
        )

    def speed(x):
        return 1.0 / lax.rsqrt(x[0] * x[0] + x[1] * x[1])

    def slip_of(m, t):
        return 1.0 / (base[m] + quad[m] * t)

    top_row = points - 1
    def early(in_sem, own_sem):
        own = pltpu.make_async_copy(cell_h, table.at[me], own_sem)
        own.start()
        loads = {}
        for i, (name, src, dst) in enumerate(
            (
                ("stretch", stretch_h, stretch),
                ("height", height_h, height),
                ("owner", owner_h, owner),
                ("target", target_h, target),
                ("face", face_h, face),
                ("prof", prof_h, prof),
                ("forc", forc_h, forc),
                ("area", area_h, area),
                ("live", live_h, live),
                ("owner_s", owner_h.at[me], owner_s),
                ("target_s", target_h.at[me], target_s),
            )
        ):
            loads[name] = pltpu.make_async_copy(src, dst, in_sem.at[i])
            loads[name].start()

        pl.semaphore_wait(barrier, 1 + (doms - 2) * ((me + doms - 1) // doms))
        own.wait()

        @pl.when(me == 0)
        def _():
            cell_copy(0, relay, cell_send, relay_recv).start()

        @pl.when(me == relay)
        def _():
            cell_copy(0, 1, relay_send, relay_recv).wait_recv()

        @pl.when(me != 0)
        def _():
            for peer in peers:

                @pl.when((me == relay) & (peer != 0))
                def _():
                    cell_copy(0, peer, relay_send, cell_recv).start()

                cell_copy(me, peer, cell_send, cell_recv).start()

        eye = lax.broadcasted_iota(jnp.int32, (blocks, blocks), 0) == lax.broadcasted_iota(
            jnp.int32, (blocks, blocks), 1
        )

        def as_column(row):
            spread = jnp.broadcast_to(row.astype(F32), (blocks, blocks))
            return jnp.sum(jnp.where(eye, spread, 0.0), axis=1, keepdims=True)

        depth = sub * half
        tall_rows = sub * (half + 1)
        row_id = lax.broadcasted_iota(jnp.int32, (tall_rows, depth), 0)
        col_id = lax.broadcasted_iota(jnp.int32, (tall_rows, depth), 1)
        shift = row_id // sub - col_id % half
        same = row_id % sub == col_id // half
        turn = jnp.where(
            same, (shift == 0).astype(F32) - (shift == 1).astype(F32), 0.0
        ).astype(BF16)

        loads["stretch"].wait()
        loads["height"].wait()
        rate = BASE_RATE + as_column(stretch[...])
        tall = height[...].astype(F32)
        step_rate = jnp.broadcast_to(rate / points, wide)
        growth = jnp.exp(step_rate)
        decay = 1.0 / growth
        first = (growth - 1.0) / (jnp.exp(jnp.broadcast_to(rate, wide)) - 1.0)
        gap_scale = 0.5 * tall * first * (1.0 + growth)
        base_scale = TIME_STEP * VISCOSITY / (first * tall * gap_scale)
        quad_scale = TIME_STEP**0.5 * KARMAN / ((growth - 1.0) * gap_scale)
        mid_first = 0.5 * (1.0 + growth)

        def grid_levels(start, base_scale, quad_scale):
            chunk = min(8, half)

            def body(i, carry):
                shrink, space = carry
                for j in range(chunk):
                    m = start + i * chunk + j
                    base[m] = base_scale * (shrink * shrink)
                    ratio = quad_scale * ((mid_first - shrink) * shrink)
                    quad[m] = ratio * ratio
                    gap[m] = space
                    shrink = shrink * decay
                    space = space * growth
                return shrink, space

            return lambda carry: lax.fori_loop(0, half // chunk, body, carry)

        shrink, space = grid_levels(0, base_scale, quad_scale)((jnp.ones(wide, F32), gap_scale))
        grid_levels(half, base_scale * growth, quad_scale * growth)((shrink, space * decay))

        for name in ("owner", "target", "face"):
            loads[name].wait()
        face_now = face[...]
        face_down = jnp.transpose(face_now.astype(F32))
        cell_ids = lax.broadcasted_iota(jnp.int32, (faces, faces), 1).astype(F32)
        for b in range(blocks):
            pick[b // 2, pl.ds(b % 2 * faces, faces), :] = (
                (cell_ids == face_down[:, b : b + 1]).astype(F32).astype(BF16)
            )
        own_row = owner[me]
        aim_row = 2 * target[me]
        terms = 4 * blocks
        widen = (
            lax.broadcasted_iota(jnp.int32, (blocks, terms), 1) // 4
            == lax.broadcasted_iota(jnp.int32, (blocks, terms), 0)
        ).astype(F32).astype(BF16)
        own_wide = jnp.dot(own_row.astype(F32).astype(BF16), widen, preferred_element_type=F32)
        aim_wide = jnp.dot(aim_row.astype(F32).astype(BF16), widen, preferred_element_type=F32)
        comp = lax.broadcasted_iota(jnp.int32, (1, terms), 1) % 2
        slot_of = (own_wide * rows + aim_wide).astype(jnp.int32) + comp
        there = (
            lax.broadcasted_iota(jnp.int32, (slots, terms), 0) == slot_of
        ).astype(F32).astype(BF16)
        place[...] = jnp.concatenate([there, there], axis=1)

        loads["prof"].wait()
        for i in range(blocks // sub):
            group = pl.ds(i * sub, sub)
            for c in range(2):
                below = None
                for part in range(2):
                    levels = prof[group, c, pl.ds(part * half, half), :].reshape(depth, faces)
                    steps = jnp.dot(turn, levels, preferred_element_type=F32)
                    for j in range(half):
                        m = part * half + j
                        step = steps[sub * j : sub * (j + 1)]
                        if j == 0 and part:
                            step += below
                        jump[m, c, group] = gap[m, group] * step
                    below = steps[depth:tall_rows]
                last[c, group] = below
        for name in ("owner_s", "target_s"):
            loads[name].wait()
        for b in range(blocks):
            row_at[b] = owner_s[0, b] * rows + 2 * target_s[0, b]
            spot_at[b] = target_s[0, b] + rows * jnp.minimum(jnp.abs(owner_s[0, b] - peers[0]), 1)
        loads["forc"].wait()
        forc32[...] = forc[...].astype(F32)
        loads["area"].wait()
        loads["live"].wait()

        slip = slip_of(0, speed((jump[0, 0], jump[0, 1])))
        r = 1.0 / (slip + 1.0)
        rest = slip * r
        fore[0] = jnp.ones(wide, F32)
        held_f[0] = r
        held_r[0] = slip
        t = [jump[0, 0], jump[0, 1]]
        w = None
        for c in range(2):
            held_t[0, c] = t[c]
        for m in range(1, top_row):
            x = (jump[m, 0], jump[m, 1])
            slip = slip_of(m, speed(x))
            if m < half:
                near = slip + growth * rest
                g = growth * r
                r = 1.0 / (near + 1.0)
            else:
                near = slip + rest
                g = r
                r = 1.0 / (near + decay)
            rest = near * r
            t = [x[c] + g * t[c] for c in range(2)]
            w = g if w is None else g * w
            held_f[m] = r
            held_r[m] = slip
            fore[m] = w
            for c in range(2):
                held_t[m, c] = t[c]
        last_rest = rest
        y, push_part, top_part = None, None, None
        for m in range(top_row - 1, -1, -1):
            r, slip = held_f[m], held_r[m]
            if y is None:
                y = [r * held_t[m, c] for c in range(2)]
                push_part = r * fore[m]
                top_part = r * decay
                brink, brink_push = y, push_part
            else:
                y = [r * (held_t[m, c] + (y[c] if m < half else decay * y[c])) for c in range(2)]
                push_part = r * (fore[m] + (push_part if m < half else decay * push_part))
                top_part = r * (top_part if m < half else decay * top_part)
            for c in range(2):
                jump[m, c] = slip * y[c]
            by_push[m] = slip * push_part
            by_top[m] = slip * top_part
        edge[0] = last_rest
        edge[1] = brink_push
        for c in range(2):
            edge[2 + c] = brink[c]
        scale[0] = growth
        scale[1] = decay

    pl.run_scoped(
        early, pltpu.SemaphoreType.DMA((11,)), pltpu.SemaphoreType.DMA(())
    )
    growth, decay = scale[0], scale[1]
    face_now = face[...]

    @pl.when(me == relay)
    def _():
        cells_of(doms - 2, cell_send, cell_recv).wait_recv()

    @pl.when(me != relay)
    def _():
        cells_of(doms - 1, cell_send, cell_recv).wait_recv()

    held[...] = table[...].astype(F32).reshape(slots, faces)
    for b in range(blocks):
        rows_of[pl.ds(2 * b, 2), :] = held[pl.ds(row_at[b], 2), :]
    edge_low, edge_high, x_top = [], [], []
    for c in range(2):
        matching = jnp.take_along_axis(
            rows_of[pl.ds(c, blocks, stride=2), :], face_now, axis=1, mode="promise_in_bounds"
        )
        excess = matching + last[c]
        push = forc32[pl.ds(c, blocks, stride=2), :] + excess
        source = TIME_STEP * PUSH_GAIN * push
        edge_low.append(gap[0] * source)
        edge_high.append(-gap[top_row] * source)
        x_top.append(jump[top_row, c] + gap[top_row] * excess)
    slip = slip_of(top_row, speed(x_top))
    share = 1.0 / (slip + edge[0])
    y_top = [
        (x_top[c] + edge_high[c] + edge[2 + c] + edge_low[c] * edge[1]) * share for c in range(2)
    ]
    x_top = [slip * y_top[c] for c in range(2)]

    def first_answer(m):
        if m == top_row:
            return x_top
        return [
            jump[m, c] + edge_low[c] * by_push[m] + y_top[c] * by_top[m] for c in range(2)
        ]

    def eliminate(m, ratio, state, ends, first):
        if first:
            x = first_answer(m)
            slip = slip_of(m, speed(x))
        else:
            x = [jump[m, c] for c in range(2)]
            slip = slip_of(m, held_r[m])
        if state is None:
            near = slip
            t = [x[c] + ends[c] for c in range(2)]
        else:
            above, h, t = state
            near = slip + above
            t = [x[c] + h * t[c] for c in range(2)]
        f = 1.0 / (near + 1.0)
        h = ratio * f
        return slip, near, f, t, (near * h, h, t)

    def forward(first):
        low, high = None, None
        for i in range(half):
            for m in (i, top_row - i):
                if m == i:
                    slip, near, f, t, low = eliminate(m, growth, low, edge_low, first)
                else:
                    slip, near, f, t, high = eliminate(m, decay, high, edge_high, first)
                held_f[m] = f
                held_s[m] = slip
                for c in range(2):
                    held_t[m, c] = t[c]
                if i == half - 1:
                    middle[m - i] = near

    def settle(m, y):
        slip = held_s[m]
        x = [slip * y[c] for c in range(2)]
        for c in range(2):
            jump[m, c] = x[c]
        held_r[m] = speed(x)

    def backward(final):
        f_high = held_f[half]
        share = 1.0 / (middle[0] + middle[1] * f_high)
        down, up = [], []
        for c in range(2):
            t_high = held_t[half, c]
            down.append((held_t[half - 1, c] + f_high * t_high) * share)
            up.append(f_high * (t_high + down[c]))
        if not final:
            settle(half - 1, down)
            settle(half, up)
        for i in range(half - 2, -1, -1):
            for m, y in ((i, down), (top_row - i, up)):
                if final and m != i:
                    continue
                f = held_f[m]
                for c in range(2):
                    y[c] = f * (held_t[m, c] + y[c])
                if not final:
                    settle(m, y)
        return down

    forward(True)

    def time_step(_, carry):
        backward(False)
        forward(False)
        return carry

    lax.fori_loop(2, STEPS, time_step, 0)
    down = backward(True)

    wall = [held_s[0] * down[c] for c in range(2)]
    wall_flux = (base[0] + quad[0] * speed(wall)) * (1.0 / TIME_STEP)
    lane = lax.broadcasted_iota(jnp.int32, live.shape, 1)
    own_live = jnp.sum(
        jnp.where(lane == me * grps + mine, live[...], 0).astype(F32), axis=1, keepdims=True
    )
    alive = lax.broadcasted_iota(jnp.int32, wide, 0).astype(F32) < own_live
    size = area[...]
    for c in range(2):
        shear = jnp.where(alive, wall_flux * wall[c], 0.0)
        shear_ref[pl.ds(c, blocks, stride=2), :] = shear
        piece = shear * size
        top = piece.astype(BF16).astype(F32)
        cells[pl.ds(c, blocks, stride=4), :] = top
        cells[pl.ds(2 + c, blocks, stride=4), :] = piece - top
    upper = lax.broadcasted_iota(jnp.int32, (8, faces), 0) < 4
    for p in range(blocks // 2):
        both = cells[pl.ds(8 * p, 8), :]
        pair = jnp.concatenate(
            [jnp.where(upper, both, 0.0), jnp.where(upper, 0.0, both)], axis=1
        ).astype(BF16)
        cells[pl.ds(8 * p, 8), :] = jnp.dot(pair, pick[p], preferred_element_type=F32)
    spots = lax.broadcasted_iota(jnp.int32, (rows // 2, faces), 0)
    sums = [jnp.zeros((rows // 2, faces), F32) for _ in range(2)]
    for b in range(blocks):
        here = spots == spot_at[b]
        for c in range(2):
            row = cells[pl.ds(4 * b + c, 1), :] + cells[pl.ds(4 * b + 2 + c, 1), :]
            sums[c] += jnp.where(here, jnp.broadcast_to(row, (rows // 2, faces)), 0.0)
    for c in range(2):
        early_out[pl.ds(c, rows // 2, stride=2), :] = sums[c]

    def force_copy(src, peer):
        return pltpu.make_async_remote_copy(
            src_ref=src,
            dst_ref=arrived.at[lax.rem(peer - me + doms, doms) - 1],
            send_sem=force_send,
            recv_sem=force_recv,
            device_id={"dom": peer},
            device_id_type=MESH,
        )

    force_copy(early_out, peers[0]).start()
    by_cell = cells[...]
    top = by_cell.astype(BF16)
    low = (by_cell - top.astype(F32)).astype(BF16)
    total = jnp.dot(
        place[...], jnp.concatenate([top, low], axis=0), preferred_element_type=F32
    )
    packed[...] = total.reshape(doms, rows, faces)
    for peer in peers[1:]:
        force_copy(packed.at[peer], peer).start()
    forces = pltpu.make_async_remote_copy(
        src_ref=packed.at[pl.ds(0, doms - 1)],
        dst_ref=arrived,
        send_sem=force_send,
        recv_sem=force_recv,
        device_id={"dom": relay},
        device_id_type=MESH,
    )
    @pl.when(me == 0)
    def _():
        cells_of(1, cell_send, relay_recv).wait_send()

    @pl.when(me != 0)
    def _():
        cells_of(doms - 1, cell_send, cell_recv).wait_send()

    @pl.when(me == relay)
    def _():
        cells_of(doms - 2, relay_send, cell_recv).wait_send()

    forces.wait_send()
    forces.wait_recv()
    result = packed[me]
    for j in range(doms - 1):
        result += arrived[j]
    force_ref[...] = result


def emit(shear_ref, force_ref, shear_out, force_out, sem):
    copies = (
        pltpu.make_async_copy(shear_ref, shear_out, sem.at[0]),
        pltpu.make_async_copy(force_ref, force_out, sem.at[1]),
    )
    for copy in copies:
        copy.start()
    for copy in copies:
        copy.wait()


def body(
    doms,
    grps,
    profile,
    forcing,
    height,
    area,
    stretch,
    face_cell,
    match_owner,
    match_block,
    live_blocks,
    cell_velocity,
):
    blocks, _, points, faces = profile.shape
    rows = 2 * cell_velocity.shape[0]
    everything = pl.BlockSpec(memory_space=pltpu.HBM)
    vmem = pl.BlockSpec(memory_space=pltpu.VMEM)
    deep = (points, blocks, faces)
    dma = pltpu.SemaphoreType.DMA
    vmem_bytes = 32 << 20
    args = (
        profile,
        forcing.reshape(2 * blocks, faces),
        height,
        area,
        stretch.reshape(1, blocks),
        face_cell,
        match_owner,
        match_block,
        live_blocks.reshape(1, -1),
        cell_velocity.reshape(rows, faces),
    )
    shear, force = pl.pallas_call(
        functools.partial(kernel, doms, grps),
        out_shape=(
            jax.ShapeDtypeStruct((2 * blocks, faces), F32),
            jax.ShapeDtypeStruct((rows, faces), F32),
        ),
        in_specs=[everything] * len(args),
        out_specs=(vmem, vmem),
        scratch_shapes=[pltpu.VMEM(arg.shape, arg.dtype) for arg in args[:-1]]
        + [
            pltpu.VMEM((doms, rows, faces), BF16),
            pltpu.VMEM((points, 2, blocks, faces), F32),
            pltpu.VMEM(deep, F32),
            pltpu.VMEM(deep, F32),
            pltpu.VMEM(deep, F32),
            pltpu.VMEM((points, 2, blocks, faces), F32),
            pltpu.VMEM(deep, F32),
            pltpu.VMEM(deep, F32),
            pltpu.VMEM(deep, F32),
            pltpu.VMEM(deep, F32),
            pltpu.VMEM(deep, F32),
            pltpu.VMEM(deep, F32),
            pltpu.VMEM((2, blocks, faces), F32),
            pltpu.VMEM((4, blocks, faces), F32),
            pltpu.VMEM((2, blocks, faces), F32),
            pltpu.VMEM((2, blocks, faces), F32),
            pltpu.VMEM((doms * rows, faces), F32),
            pltpu.VMEM((2 * blocks, faces), F32),
            pltpu.SMEM((1, blocks), jnp.int32),
            pltpu.SMEM((1, blocks), jnp.int32),
            pltpu.SMEM((blocks,), jnp.int32),
            pltpu.SMEM((blocks,), jnp.int32),
            pltpu.VMEM((rows, faces), F32),
            pltpu.VMEM((blocks // 2, 2 * faces, faces), BF16),
            pltpu.VMEM((doms * rows, 8 * blocks), BF16),
            pltpu.VMEM((4 * blocks, faces), F32),
            pltpu.VMEM((doms, rows, faces), F32),
            pltpu.VMEM((doms - 1, rows, faces), F32),
            pltpu.VMEM((2 * blocks, faces), F32),
            dma,
            dma,
            dma,
            dma,
            dma,
            dma,
        ],
        compiler_params=pltpu.CompilerParams(
            collective_id=0, has_side_effects=True, vmem_limit_bytes=vmem_bytes
        ),
        name="wall_model",
    )(*[pltpu.with_memory_space_constraint(x, pltpu.HBM) for x in args])
    shear, force = pl.pallas_call(
        emit,
        out_shape=(
            jax.ShapeDtypeStruct(shear.shape, F32),
            jax.ShapeDtypeStruct(force.shape, F32),
        ),
        in_specs=[pl.BlockSpec(memory_space=pl.ANY)] * 2,
        out_specs=(pl.BlockSpec(memory_space=pl.ANY),) * 2,
        scratch_shapes=[dma((2,))],
        compiler_params=pltpu.CompilerParams(vmem_limit_bytes=1 << 20),
        name="emit",
    )(shear, force)
    return (
        shear.reshape(blocks, 2, faces),
        force.reshape(cell_velocity.shape[0], 2, faces),
    )


def solution(mesh):
    in_specs = (
        P(("dom", "grp"), None, None, None),
        P(("dom", "grp"), None, None),
        P(("dom", "grp"), None),
        P(("dom", "grp"), None),
        P(("dom", "grp")),
        P(("dom", "grp"), None),
        P(None, "grp", None),
        P(None, "grp", None),
        P(),
        P(("dom", "grp"), None, None),
    )
    out_specs = (P(("dom", "grp"), None, None), P(("dom", "grp"), None, None))
    step = functools.partial(body, mesh.shape["dom"], mesh.shape["grp"])
    return jax.shard_map(step, mesh=mesh, in_specs=in_specs, out_specs=out_specs, check_vma=False)
```

```python
import functools

import jax
import jax.numpy as jnp
from jax import lax
from jax.experimental import pallas as pl
from jax.experimental.pallas import tpu as pltpu
from jax.sharding import PartitionSpec as P

STEPS = 4
VISCOSITY = 0.005
KARMAN = 0.41
TIME_STEP = 2.0
PUSH_GAIN = 0.5
BASE_RATE = 1.5
MESH = pl.DeviceIdType.MESH
F32 = jnp.float32
BF16 = jnp.bfloat16


def kernel(
    doms,
    grps,
    prof_h,
    forc_h,
    height_h,
    area_h,
    stretch_h,
    face_h,
    owner_h,
    target_h,
    live_h,
    cell_h,
    shear_ref,
    force_ref,
    prof,
    forc,
    height,
    area,
    stretch,
    face,
    owner,
    target,
    live,
    table,
    jump,
    held_f,
    held_r,
    held_s,
    held_t,
    fore,
    by_push,
    by_top,
    base,
    quad,
    gap,
    last,
    edge,
    middle,
    scale,
    held,
    rows_of,
    owner_s,
    target_s,
    row_at,
    spot_at,
    early_out,
    pick,
    place,
    cells,
    packed,
    arrived,
    forc32,
    cell_send,
    cell_recv,
    relay_send,
    relay_recv,
    force_send,
    force_recv,
):
    blocks, _, points, faces = prof.shape
    rows = cell_h.shape[0]
    slots = doms * rows
    half = points // 2
    sub = 8
    relay = min(2, doms - 1)
    me = lax.axis_index("dom")
    mine = lax.axis_index("grp")
    wide = (blocks, faces)

    high = (2 * me) // doms
    odd = (1 - high) * (me % 2) if doms % 2 == 0 else 0
    spot = high * me + (1 - high) * (doms - 1 - me + odd)

    def peer_at(k):
        step = k + (k - spot + doms) // doms
        peer = high * step + (1 - high) * (doms - 1 - step)
        return peer + odd * (1 - 2 * (peer % 2))

    barrier = pltpu.get_barrier_semaphore()
    first = doms // 2 - 1
    for j in list(range(first, doms)) + list(range(1, first)):
        peer = lax.rem(me + j, doms)

        @pl.when((peer != 0) | (me == relay))
        def _():
            pl.semaphore_signal(barrier, inc=1, device_id={"dom": peer}, device_id_type=MESH)

    peers = [peer_at(k) for k in range(doms - 1)]

    def cell_copy(slot, peer, send, recv):
        return pltpu.make_async_remote_copy(
            src_ref=table.at[slot],
            dst_ref=table.at[slot],
            send_sem=send,
            recv_sem=recv,
            device_id={"dom": peer},
            device_id_type=MESH,
        )

    def cells_of(count, send, recv):
        return pltpu.make_async_remote_copy(
            src_ref=table.at[pl.ds(0, count)],
            dst_ref=table.at[pl.ds(0, count)],
            send_sem=send,
            recv_sem=recv,
            device_id={"dom": relay},
            device_id_type=MESH,
        )

    def speed(x):
        return 1.0 / lax.rsqrt(x[0] * x[0] + x[1] * x[1])

    def slip_of(m, t):
        return 1.0 / (base[m] + quad[m] * t)

    top_row = points - 1
    def early(in_sem, own_sem):
        own = pltpu.make_async_copy(cell_h, table.at[me], own_sem)
        own.start()
        loads = {}
        for i, (name, src, dst) in enumerate(
            (
                ("stretch", stretch_h, stretch),
                ("height", height_h, height),
                ("owner", owner_h, owner),
                ("target", target_h, target),
                ("face", face_h, face),
                ("prof", prof_h, prof),
                ("forc", forc_h, forc),
                ("area", area_h, area),
                ("live", live_h, live),
                ("owner_s", owner_h.at[me], owner_s),
                ("target_s", target_h.at[me], target_s),
            )
        ):
            loads[name] = pltpu.make_async_copy(src, dst, in_sem.at[i])
            loads[name].start()

        pl.semaphore_wait(barrier, 1 + (doms - 2) * ((me + doms - 1) // doms))
        own.wait()

        @pl.when(me == 0)
        def _():
            cell_copy(0, relay, cell_send, relay_recv).start()

        @pl.when(me == relay)
        def _():
            cell_copy(0, 1, relay_send, relay_recv).wait_recv()

        @pl.when(me != 0)
        def _():
            for peer in peers:

                @pl.when((me == relay) & (peer != 0))
                def _():
                    cell_copy(0, peer, relay_send, cell_recv).start()

                cell_copy(me, peer, cell_send, cell_recv).start()

        eye = lax.broadcasted_iota(jnp.int32, (blocks, blocks), 0) == lax.broadcasted_iota(
            jnp.int32, (blocks, blocks), 1
        )

        def as_column(row):
            spread = jnp.broadcast_to(row.astype(F32), (blocks, blocks))
            return jnp.sum(jnp.where(eye, spread, 0.0), axis=1, keepdims=True)

        depth = sub * half
        tall_rows = sub * (half + 1)
        row_id = lax.broadcasted_iota(jnp.int32, (tall_rows, depth), 0)
        col_id = lax.broadcasted_iota(jnp.int32, (tall_rows, depth), 1)
        shift = row_id // sub - col_id % half
        same = row_id % sub == col_id // half
        turn = jnp.where(
            same, (shift == 0).astype(F32) - (shift == 1).astype(F32), 0.0
        ).astype(BF16)

        loads["stretch"].wait()
        loads["height"].wait()
        rate = BASE_RATE + as_column(stretch[...])
        tall = height[...].astype(F32)
        step_rate = jnp.broadcast_to(rate / points, wide)
        growth = jnp.exp(step_rate)
        decay = 1.0 / growth
        first = (growth - 1.0) / (jnp.exp(jnp.broadcast_to(rate, wide)) - 1.0)
        gap_scale = 0.5 * tall * first * (1.0 + growth)
        base_scale = TIME_STEP * VISCOSITY / (first * tall * gap_scale)
        quad_scale = TIME_STEP**0.5 * KARMAN / ((growth - 1.0) * gap_scale)
        mid_first = 0.5 * (1.0 + growth)

        def grid_levels(start, base_scale, quad_scale):
            chunk = min(8, half)

            def body(i, carry):
                shrink, space = carry
                for j in range(chunk):
                    m = start + i * chunk + j
                    base[m] = base_scale * (shrink * shrink)
                    ratio = quad_scale * ((mid_first - shrink) * shrink)
                    quad[m] = ratio * ratio
                    gap[m] = space
                    shrink = shrink * decay
                    space = space * growth
                return shrink, space

            return lambda carry: lax.fori_loop(0, half // chunk, body, carry)

        shrink, space = grid_levels(0, base_scale, quad_scale)((jnp.ones(wide, F32), gap_scale))
        grid_levels(half, base_scale * growth, quad_scale * growth)((shrink, space * decay))

        for name in ("owner", "target", "face"):
            loads[name].wait()
        face_now = face[...]
        face_down = jnp.transpose(face_now.astype(F32))
        cell_ids = lax.broadcasted_iota(jnp.int32, (faces, faces), 1).astype(F32)
        for b in range(blocks):
            pick[b // 2, pl.ds(b % 2 * faces, faces), :] = (
                (cell_ids == face_down[:, b : b + 1]).astype(F32).astype(BF16)
            )
        own_row = owner[me]
        aim_row = 2 * target[me]
        terms = 4 * blocks
        widen = (
            lax.broadcasted_iota(jnp.int32, (blocks, terms), 1) // 4
            == lax.broadcasted_iota(jnp.int32, (blocks, terms), 0)
        ).astype(F32).astype(BF16)
        own_wide = jnp.dot(own_row.astype(F32).astype(BF16), widen, preferred_element_type=F32)
        aim_wide = jnp.dot(aim_row.astype(F32).astype(BF16), widen, preferred_element_type=F32)
        comp = lax.broadcasted_iota(jnp.int32, (1, terms), 1) % 2
        slot_of = (own_wide * rows + aim_wide).astype(jnp.int32) + comp
        there = (
            lax.broadcasted_iota(jnp.int32, (slots, terms), 0) == slot_of
        ).astype(F32).astype(BF16)
        place[...] = jnp.concatenate([there, there], axis=1)

        loads["prof"].wait()
        for i in range(blocks // sub):
            group = pl.ds(i * sub, sub)
            for c in range(2):
                below = None
                for part in range(2):
                    levels = prof[group, c, pl.ds(part * half, half), :].reshape(depth, faces)
                    steps = jnp.dot(turn, levels, preferred_element_type=F32)
                    for j in range(half):
                        m = part * half + j
                        step = steps[sub * j : sub * (j + 1)]
                        if j == 0 and part:
                            step += below
                        jump[m, c, group] = gap[m, group] * step
                    below = steps[depth:tall_rows]
                last[c, group] = below
        for name in ("owner_s", "target_s"):
            loads[name].wait()
        for b in range(blocks):
            row_at[b] = owner_s[0, b] * rows + 2 * target_s[0, b]
            spot_at[b] = target_s[0, b] + rows * jnp.minimum(jnp.abs(owner_s[0, b] - peers[0]), 1)
        loads["forc"].wait()
        forc32[...] = forc[...].astype(F32)
        loads["area"].wait()
        loads["live"].wait()

        slip = slip_of(0, speed((jump[0, 0], jump[0, 1])))
        r = 1.0 / (slip + 1.0)
        rest = slip * r
        fore[0] = jnp.ones(wide, F32)
        held_f[0] = r
        held_r[0] = slip
        t = [jump[0, 0], jump[0, 1]]
        w = None
        for c in range(2):
            held_t[0, c] = t[c]
        for m in range(1, top_row):
            x = (jump[m, 0], jump[m, 1])
            slip = slip_of(m, speed(x))
            if m < half:
                near = slip + growth * rest
                g = growth * r
                r = 1.0 / (near + 1.0)
            else:
                near = slip + rest
                g = r
                r = 1.0 / (near + decay)
            rest = near * r
            t = [x[c] + g * t[c] for c in range(2)]
            w = g if w is None else g * w
            held_f[m] = r
            held_r[m] = slip
            fore[m] = w
            for c in range(2):
                held_t[m, c] = t[c]
        last_rest = rest
        y, push_part, top_part = None, None, None
        for m in range(top_row - 1, -1, -1):
            r, slip = held_f[m], held_r[m]
            if y is None:
                y = [r * held_t[m, c] for c in range(2)]
                push_part = r * fore[m]
                top_part = r * decay
                brink, brink_push = y, push_part
            else:
                y = [r * (held_t[m, c] + (y[c] if m < half else decay * y[c])) for c in range(2)]
                push_part = r * (fore[m] + (push_part if m < half else decay * push_part))
                top_part = r * (top_part if m < half else decay * top_part)
            for c in range(2):
                jump[m, c] = slip * y[c]
            by_push[m] = slip * push_part
            by_top[m] = slip * top_part
        edge[0] = last_rest
        edge[1] = brink_push
        for c in range(2):
            edge[2 + c] = brink[c]
        scale[0] = growth
        scale[1] = decay

    pl.run_scoped(
        early, pltpu.SemaphoreType.DMA((11,)), pltpu.SemaphoreType.DMA(())
    )
    growth, decay = scale[0], scale[1]
    face_now = face[...]

    @pl.when(me == relay)
    def _():
        cells_of(doms - 2, cell_send, cell_recv).wait_recv()

    @pl.when(me != relay)
    def _():
        cells_of(doms - 1, cell_send, cell_recv).wait_recv()

    held[pl.ds(0, slots), :] = table[...].astype(F32).reshape(slots, faces)
    for b in range(blocks):
        rows_of[pl.ds(2 * b, 2), :] = held[pl.ds(row_at[b], 2), :]
    edge_low, edge_high, x_top = [], [], []
    for c in range(2):
        matching = jnp.take_along_axis(
            rows_of[pl.ds(c, blocks, stride=2), :], face_now, axis=1, mode="promise_in_bounds"
        )
        excess = matching + last[c]
        push = forc32[pl.ds(c, blocks, stride=2), :] + excess
        source = TIME_STEP * PUSH_GAIN * push
        edge_low.append(gap[0] * source)
        edge_high.append(-gap[top_row] * source)
        x_top.append(jump[top_row, c] + gap[top_row] * excess)
    slip = slip_of(top_row, speed(x_top))
    share = 1.0 / (slip + edge[0])
    y_top = [
        (x_top[c] + edge_high[c] + edge[2 + c] + edge_low[c] * edge[1]) * share for c in range(2)
    ]
    x_top = [slip * y_top[c] for c in range(2)]

    def first_answer(m):
        if m == top_row:
            return x_top
        return [
            jump[m, c] + edge_low[c] * by_push[m] + y_top[c] * by_top[m] for c in range(2)
        ]

    def eliminate(m, ratio, state, ends, first):
        if first:
            x = first_answer(m)
            slip = slip_of(m, speed(x))
        else:
            x = [jump[m, c] for c in range(2)]
            slip = slip_of(m, held_r[m])
        if state is None:
            near = slip
            t = [x[c] + ends[c] for c in range(2)]
        else:
            above, h, t = state
            near = slip + above
            t = [x[c] + h * t[c] for c in range(2)]
        f = 1.0 / (near + 1.0)
        h = ratio * f
        return slip, near, f, t, (near * h, h, t)

    def forward(first):
        low, high = None, None
        for i in range(half):
            for m in (i, top_row - i):
                if m == i:
                    slip, near, f, t, low = eliminate(m, growth, low, edge_low, first)
                else:
                    slip, near, f, t, high = eliminate(m, decay, high, edge_high, first)
                held_f[m] = f
                held_s[m] = slip
                for c in range(2):
                    held_t[m, c] = t[c]
                if i == half - 1:
                    middle[m - i] = near

    def settle(m, y):
        slip = held_s[m]
        x = [slip * y[c] for c in range(2)]
        for c in range(2):
            jump[m, c] = x[c]
        held_r[m] = speed(x)

    def backward(final):
        f_high = held_f[half]
        share = 1.0 / (middle[0] + middle[1] * f_high)
        down, up = [], []
        for c in range(2):
            t_high = held_t[half, c]
            down.append((held_t[half - 1, c] + f_high * t_high) * share)
            up.append(f_high * (t_high + down[c]))
        if not final:
            settle(half - 1, down)
            settle(half, up)
        for i in range(half - 2, -1, -1):
            for m, y in ((i, down), (top_row - i, up)):
                if final and m != i:
                    continue
                f = held_f[m]
                for c in range(2):
                    y[c] = f * (held_t[m, c] + y[c])
                if not final:
                    settle(m, y)
        return down

    forward(True)

    def time_step(_, carry):
        backward(False)
        forward(False)
        return carry

    lax.fori_loop(2, STEPS, time_step, 0)
    down = backward(True)

    wall = [held_s[0] * down[c] for c in range(2)]
    wall_flux = (base[0] + quad[0] * speed(wall)) * (1.0 / TIME_STEP)
    lane = lax.broadcasted_iota(jnp.int32, live.shape, 1)
    own_live = jnp.sum(
        jnp.where(lane == me * grps + mine, live[...], 0).astype(F32), axis=1, keepdims=True
    )
    alive = lax.broadcasted_iota(jnp.int32, wide, 0).astype(F32) < own_live
    size = area[...]
    for c in range(2):
        shear = jnp.where(alive, wall_flux * wall[c], 0.0)
        shear_ref[pl.ds(c, blocks, stride=2), :] = shear
        piece = shear * size
        top = piece.astype(BF16).astype(F32)
        cells[pl.ds(c, blocks, stride=4), :] = top
        cells[pl.ds(2 + c, blocks, stride=4), :] = piece - top
    upper = lax.broadcasted_iota(jnp.int32, (8, faces), 0) < 4
    for p in range(blocks // 2):
        both = cells[pl.ds(8 * p, 8), :]
        pair = jnp.concatenate(
            [jnp.where(upper, both, 0.0), jnp.where(upper, 0.0, both)], axis=1
        ).astype(BF16)
        cells[pl.ds(8 * p, 8), :] = jnp.dot(pair, pick[p], preferred_element_type=F32)
    spots = lax.broadcasted_iota(jnp.int32, (rows // 2, faces), 0)
    sums = [jnp.zeros((rows // 2, faces), F32) for _ in range(2)]
    for b in range(blocks):
        here = spots == spot_at[b]
        for c in range(2):
            row = cells[pl.ds(4 * b + c, 1), :] + cells[pl.ds(4 * b + 2 + c, 1), :]
            sums[c] += jnp.where(here, jnp.broadcast_to(row, (rows // 2, faces)), 0.0)
    for c in range(2):
        early_out[pl.ds(c, rows // 2, stride=2), :] = sums[c]

    def force_copy(src, peer):
        return pltpu.make_async_remote_copy(
            src_ref=src,
            dst_ref=arrived.at[lax.rem(peer - me + doms, doms) - 1],
            send_sem=force_send,
            recv_sem=force_recv,
            device_id={"dom": peer},
            device_id_type=MESH,
        )

    force_copy(early_out.at[pl.ds(0, rows)], peers[0]).start()
    by_cell = cells[pl.ds(0, 4 * blocks), :]
    top = by_cell.astype(BF16)
    low = (by_cell - top.astype(F32)).astype(BF16)
    total = jnp.dot(
        place[...], jnp.concatenate([top, low], axis=0), preferred_element_type=F32
    )
    packed[...] = total.reshape(doms, rows, faces)
    for peer in peers[1:]:
        force_copy(packed.at[peer], peer).start()
    forces = pltpu.make_async_remote_copy(
        src_ref=packed.at[pl.ds(0, doms - 1)],
        dst_ref=arrived,
        send_sem=force_send,
        recv_sem=force_recv,
        device_id={"dom": relay},
        device_id_type=MESH,
    )
    @pl.when(me == 0)
    def _():
        cells_of(1, cell_send, relay_recv).wait_send()

    @pl.when(me != 0)
    def _():
        cells_of(doms - 1, cell_send, cell_recv).wait_send()

    @pl.when(me == relay)
    def _():
        cells_of(doms - 2, relay_send, cell_recv).wait_send()

    forces.wait_send()
    forces.wait_recv()
    result = packed[me]
    for j in range(doms - 1):
        result += arrived[j]
    force_ref[...] = result


def emit(shear_ref, force_ref, shear_out, force_out, sem):
    copies = (
        pltpu.make_async_copy(shear_ref, shear_out, sem.at[0]),
        pltpu.make_async_copy(force_ref, force_out, sem.at[1]),
    )
    for copy in copies:
        copy.start()
    for copy in copies:
        copy.wait()


def body(
    doms,
    grps,
    profile,
    forcing,
    height,
    area,
    stretch,
    face_cell,
    match_owner,
    match_block,
    live_blocks,
    cell_velocity,
):
    blocks, _, points, faces = profile.shape
    rows = 2 * cell_velocity.shape[0]
    everything = pl.BlockSpec(memory_space=pltpu.HBM)
    vmem = pl.BlockSpec(memory_space=pltpu.VMEM)
    deep = (points, blocks, faces)
    dma = pltpu.SemaphoreType.DMA
    vmem_bytes = 32 << 20
    args = (
        profile,
        forcing.reshape(2 * blocks, faces),
        height,
        area,
        stretch.reshape(1, blocks),
        face_cell,
        match_owner,
        match_block,
        live_blocks.reshape(1, -1),
        cell_velocity.reshape(rows, faces),
    )
    shear, force = pl.pallas_call(
        functools.partial(kernel, doms, grps),
        out_shape=(
            jax.ShapeDtypeStruct((2 * blocks, faces), F32),
            jax.ShapeDtypeStruct((rows, faces), F32),
        ),
        in_specs=[everything] * len(args),
        out_specs=(vmem, vmem),
        scratch_shapes=[pltpu.VMEM(arg.shape, arg.dtype) for arg in args[:-1]]
        + [
            pltpu.VMEM((doms, rows, faces), BF16),
            pltpu.VMEM((points, 2, blocks, faces), F32),
            pltpu.VMEM(deep, F32),
            pltpu.VMEM(deep, F32),
            pltpu.VMEM(deep, F32),
            pltpu.VMEM((points, 2, blocks, faces), F32),
            pltpu.VMEM(deep, F32),
            pltpu.VMEM(deep, F32),
            pltpu.VMEM(deep, F32),
            pltpu.VMEM(deep, F32),
            pltpu.VMEM(deep, F32),
            pltpu.VMEM(deep, F32),
            pltpu.VMEM((2, blocks, faces), F32),
            pltpu.VMEM((4, blocks, faces), F32),
            pltpu.VMEM((2, blocks, faces), F32),
            pltpu.VMEM((2, blocks, faces), F32),
            pltpu.VMEM((doms * rows + 8, faces), F32),
            pltpu.VMEM((2 * blocks + 8, faces), F32),
            pltpu.SMEM((1, blocks), jnp.int32),
            pltpu.SMEM((1, blocks), jnp.int32),
            pltpu.SMEM((blocks,), jnp.int32),
            pltpu.SMEM((blocks,), jnp.int32),
            pltpu.VMEM((rows + 16, faces), F32),
            pltpu.VMEM((blocks // 2, 2 * faces, faces), BF16),
            pltpu.VMEM((doms * rows, 8 * blocks), BF16),
            pltpu.VMEM((4 * blocks + 8, faces), F32),
            pltpu.VMEM((doms, rows, faces), F32),
            pltpu.VMEM((doms - 1, rows, faces), F32),
            pltpu.VMEM((2 * blocks, faces), F32),
            dma,
            dma,
            dma,
            dma,
            dma,
            dma,
        ],
        compiler_params=pltpu.CompilerParams(
            collective_id=0, has_side_effects=True, vmem_limit_bytes=vmem_bytes
        ),
        name="wall_model",
    )(*[pltpu.with_memory_space_constraint(x, pltpu.HBM) for x in args])
    shear, force = pl.pallas_call(
        emit,
        out_shape=(
            jax.ShapeDtypeStruct(shear.shape, F32),
            jax.ShapeDtypeStruct(force.shape, F32),
        ),
        in_specs=[pl.BlockSpec(memory_space=pl.ANY)] * 2,
        out_specs=(pl.BlockSpec(memory_space=pl.ANY),) * 2,
        scratch_shapes=[dma((2,))],
        compiler_params=pltpu.CompilerParams(vmem_limit_bytes=1 << 20),
        name="emit",
    )(shear, force)
    return (
        shear.reshape(blocks, 2, faces),
        force.reshape(cell_velocity.shape[0], 2, faces),
    )


def solution(mesh):
    in_specs = (
        P(("dom", "grp"), None, None, None),
        P(("dom", "grp"), None, None),
        P(("dom", "grp"), None),
        P(("dom", "grp"), None),
        P(("dom", "grp")),
        P(("dom", "grp"), None),
        P(None, "grp", None),
        P(None, "grp", None),
        P(),
        P(("dom", "grp"), None, None),
    )
    out_specs = (P(("dom", "grp"), None, None), P(("dom", "grp"), None, None))
    step = functools.partial(body, mesh.shape["dom"], mesh.shape["grp"])
    return jax.shard_map(step, mesh=mesh, in_specs=in_specs, out_specs=out_specs, check_vma=False)
```

```python
import functools

import jax
import jax.numpy as jnp
from jax import lax
from jax.experimental import pallas as pl
from jax.experimental.pallas import tpu as pltpu
from jax.sharding import PartitionSpec as P

STEPS = 4
VISCOSITY = 0.005
KARMAN = 0.41
TIME_STEP = 2.0
PUSH_GAIN = 0.5
BASE_RATE = 1.5
MESH = pl.DeviceIdType.MESH
F32 = jnp.float32
BF16 = jnp.bfloat16


def kernel(
    doms,
    grps,
    prof_h,
    forc_h,
    height_h,
    area_h,
    stretch_h,
    face_h,
    owner_h,
    target_h,
    live_h,
    cell_h,
    shear_ref,
    force_ref,
    prof,
    forc,
    height,
    area,
    stretch,
    face,
    owner,
    target,
    live,
    table,
    jump,
    held_f,
    held_r,
    held_s,
    held_t,
    fore,
    by_push,
    by_top,
    base,
    quad,
    gap,
    last,
    edge,
    middle,
    scale,
    held,
    rows_of,
    owner_s,
    target_s,
    row_at,
    spot_at,
    early_out,
    pick,
    place,
    cells,
    packed,
    arrived,
    forc32,
    cell_send,
    cell_recv,
    relay_send,
    relay_recv,
    force_send,
    force_recv,
):
    blocks, _, points, faces = prof.shape
    rows = cell_h.shape[0]
    slots = doms * rows
    half = points // 2
    sub = 8
    relay = min(2, doms - 1)
    me = lax.axis_index("dom")
    mine = lax.axis_index("grp")
    wide = (blocks, faces)

    high = (2 * me) // doms
    odd = (1 - high) * (me % 2) if doms % 2 == 0 else 0
    spot = high * me + (1 - high) * (doms - 1 - me + odd)

    def peer_at(k):
        step = k + (k - spot + doms) // doms
        peer = high * step + (1 - high) * (doms - 1 - step)
        return peer + odd * (1 - 2 * (peer % 2))

    barrier = pltpu.get_barrier_semaphore()
    first = doms // 2 - 1
    for j in list(range(first, doms)) + list(range(1, first)):
        peer = lax.rem(me + j, doms)

        @pl.when((peer != 0) | (me == relay))
        def _():
            pl.semaphore_signal(barrier, inc=1, device_id={"dom": peer}, device_id_type=MESH)

    peers = [peer_at(k) for k in range(doms - 1)]
    lands = [lax.rem(peer - me + doms, doms) - 1 for peer in peers]

    def cell_copy(slot, peer, send, recv):
        return pltpu.make_async_remote_copy(
            src_ref=table.at[slot],
            dst_ref=table.at[slot],
            send_sem=send,
            recv_sem=recv,
            device_id={"dom": peer},
            device_id_type=MESH,
        )

    def cells_of(count, send, recv):
        return pltpu.make_async_remote_copy(
            src_ref=table.at[pl.ds(0, count)],
            dst_ref=table.at[pl.ds(0, count)],
            send_sem=send,
            recv_sem=recv,
            device_id={"dom": relay},
            device_id_type=MESH,
        )

    def speed(x):
        return 1.0 / lax.rsqrt(x[0] * x[0] + x[1] * x[1])

    def slip_of(m, t):
        return 1.0 / (base[m] + quad[m] * t)

    top_row = points - 1
    def early(in_sem, own_sem):
        own = pltpu.make_async_copy(cell_h, table.at[me], own_sem)
        own.start()
        loads = {}
        for i, (name, src, dst) in enumerate(
            (
                ("stretch", stretch_h, stretch),
                ("height", height_h, height),
                ("owner", owner_h, owner),
                ("target", target_h, target),
                ("face", face_h, face),
                ("prof", prof_h, prof),
                ("forc", forc_h, forc),
                ("area", area_h, area),
                ("live", live_h, live),
                ("owner_s", owner_h.at[me], owner_s),
                ("target_s", target_h.at[me], target_s),
            )
        ):
            loads[name] = pltpu.make_async_copy(src, dst, in_sem.at[i])
            loads[name].start()

        pl.semaphore_wait(barrier, 1 + (doms - 2) * ((me + doms - 1) // doms))
        own.wait()

        @pl.when(me == 0)
        def _():
            cell_copy(0, relay, cell_send, relay_recv).start()

        @pl.when(me == relay)
        def _():
            cell_copy(0, 1, relay_send, relay_recv).wait_recv()

        @pl.when(me != 0)
        def _():
            for peer in peers:

                @pl.when((me == relay) & (peer != 0))
                def _():
                    cell_copy(0, peer, relay_send, cell_recv).start()

                cell_copy(me, peer, cell_send, cell_recv).start()

        eye = lax.broadcasted_iota(jnp.int32, (blocks, blocks), 0) == lax.broadcasted_iota(
            jnp.int32, (blocks, blocks), 1
        )

        def as_column(row):
            spread = jnp.broadcast_to(row.astype(F32), (blocks, blocks))
            return jnp.sum(jnp.where(eye, spread, 0.0), axis=1, keepdims=True)

        depth = sub * half
        tall_rows = sub * (half + 1)
        row_id = lax.broadcasted_iota(jnp.int32, (tall_rows, depth), 0)
        col_id = lax.broadcasted_iota(jnp.int32, (tall_rows, depth), 1)
        shift = row_id // sub - col_id % half
        same = row_id % sub == col_id // half
        turn = jnp.where(
            same, (shift == 0).astype(F32) - (shift == 1).astype(F32), 0.0
        ).astype(BF16)

        loads["stretch"].wait()
        loads["height"].wait()
        rate = BASE_RATE + as_column(stretch[...])
        tall = height[...].astype(F32)
        step_rate = jnp.broadcast_to(rate / points, wide)
        growth = jnp.exp(step_rate)
        decay = 1.0 / growth
        first = (growth - 1.0) / (jnp.exp(jnp.broadcast_to(rate, wide)) - 1.0)
        gap_scale = 0.5 * tall * first * (1.0 + growth)
        base_scale = TIME_STEP * VISCOSITY / (first * tall * gap_scale)
        quad_scale = TIME_STEP**0.5 * KARMAN / ((growth - 1.0) * gap_scale)
        mid_first = 0.5 * (1.0 + growth)

        def grid_levels(start, base_scale, quad_scale):
            chunk = min(8, half)

            def body(i, carry):
                shrink, space = carry
                for j in range(chunk):
                    m = start + i * chunk + j
                    base[m] = base_scale * (shrink * shrink)
                    ratio = quad_scale * ((mid_first - shrink) * shrink)
                    quad[m] = ratio * ratio
                    gap[m] = space
                    shrink = shrink * decay
                    space = space * growth
                return shrink, space

            return lambda carry: lax.fori_loop(0, half // chunk, body, carry)

        shrink, space = grid_levels(0, base_scale, quad_scale)((jnp.ones(wide, F32), gap_scale))
        grid_levels(half, base_scale * growth, quad_scale * growth)((shrink, space * decay))

        for name in ("owner", "target", "face"):
            loads[name].wait()
        face_now = face[...]
        face_down = jnp.transpose(face_now.astype(F32))
        cell_ids = lax.broadcasted_iota(jnp.int32, (faces, faces), 1).astype(F32)
        for b in range(blocks):
            pick[b // 2, pl.ds(b % 2 * faces, faces), :] = (
                (cell_ids == face_down[:, b : b + 1]).astype(F32).astype(BF16)
            )
        own_row = owner[me]
        aim_row = 2 * target[me]
        terms = 4 * blocks
        widen = (
            lax.broadcasted_iota(jnp.int32, (blocks, terms), 1) // 4
            == lax.broadcasted_iota(jnp.int32, (blocks, terms), 0)
        ).astype(F32).astype(BF16)
        own_wide = jnp.dot(own_row.astype(F32).astype(BF16), widen, preferred_element_type=F32)
        aim_wide = jnp.dot(aim_row.astype(F32).astype(BF16), widen, preferred_element_type=F32)
        comp = lax.broadcasted_iota(jnp.int32, (1, terms), 1) % 2
        slot_of = (own_wide * rows + aim_wide).astype(jnp.int32) + comp
        there = (
            lax.broadcasted_iota(jnp.int32, (slots, terms), 0) == slot_of
        ).astype(F32).astype(BF16)
        place[...] = jnp.concatenate([there, there], axis=1)

        loads["prof"].wait()
        for i in range(blocks // sub):
            group = pl.ds(i * sub, sub)
            for c in range(2):
                below = None
                for part in range(2):
                    levels = prof[group, c, pl.ds(part * half, half), :].reshape(depth, faces)
                    steps = jnp.dot(turn, levels, preferred_element_type=F32)
                    for j in range(half):
                        m = part * half + j
                        step = steps[sub * j : sub * (j + 1)]
                        if j == 0 and part:
                            step += below
                        jump[m, c, group] = gap[m, group] * step
                    below = steps[depth:tall_rows]
                last[c, group] = below
        for name in ("owner_s", "target_s"):
            loads[name].wait()
        for b in range(blocks):
            row_at[b] = owner_s[0, b] * rows + 2 * target_s[0, b]
            spot_at[b] = target_s[0, b] + rows * jnp.minimum(jnp.abs(owner_s[0, b] - peers[0]), 1)
        loads["forc"].wait()
        forc32[...] = forc[...].astype(F32)
        loads["area"].wait()
        loads["live"].wait()

        slip = slip_of(0, speed((jump[0, 0], jump[0, 1])))
        r = 1.0 / (slip + 1.0)
        rest = slip * r
        fore[0] = jnp.ones(wide, F32)
        held_f[0] = r
        held_r[0] = slip
        t = [jump[0, 0], jump[0, 1]]
        w = None
        for c in range(2):
            held_t[0, c] = t[c]
        for m in range(1, top_row):
            x = (jump[m, 0], jump[m, 1])
            slip = slip_of(m, speed(x))
            if m < half:
                near = slip + growth * rest
                g = growth * r
                r = 1.0 / (near + 1.0)
            else:
                near = slip + rest
                g = r
                r = 1.0 / (near + decay)
            rest = near * r
            t = [x[c] + g * t[c] for c in range(2)]
            w = g if w is None else g * w
            held_f[m] = r
            held_r[m] = slip
            fore[m] = w
            for c in range(2):
                held_t[m, c] = t[c]
        last_rest = rest
        y, push_part, top_part = None, None, None
        for m in range(top_row - 1, -1, -1):
            r, slip = held_f[m], held_r[m]
            if y is None:
                y = [r * held_t[m, c] for c in range(2)]
                push_part = r * fore[m]
                top_part = r * decay
                brink, brink_push = y, push_part
            else:
                y = [r * (held_t[m, c] + (y[c] if m < half else decay * y[c])) for c in range(2)]
                push_part = r * (fore[m] + (push_part if m < half else decay * push_part))
                top_part = r * (top_part if m < half else decay * top_part)
            for c in range(2):
                jump[m, c] = slip * y[c]
            by_push[m] = slip * push_part
            by_top[m] = slip * top_part
        edge[0] = last_rest
        edge[1] = brink_push
        for c in range(2):
            edge[2 + c] = brink[c]
        scale[0] = growth
        scale[1] = decay

    pl.run_scoped(
        early, pltpu.SemaphoreType.DMA((11,)), pltpu.SemaphoreType.DMA(())
    )
    growth, decay = scale[0], scale[1]
    face_now = face[...]

    @pl.when(me == relay)
    def _():
        cells_of(doms - 2, cell_send, cell_recv).wait_recv()

    @pl.when(me != relay)
    def _():
        cells_of(doms - 1, cell_send, cell_recv).wait_recv()

    held[pl.ds(0, slots), :] = table[...].astype(F32).reshape(slots, faces)
    for b in range(blocks):
        rows_of[pl.ds(2 * b, 2), :] = held[pl.ds(row_at[b], 2), :]
    edge_low, edge_high, x_top = [], [], []
    for c in range(2):
        matching = jnp.take_along_axis(
            rows_of[pl.ds(c, blocks, stride=2), :], face_now, axis=1, mode="promise_in_bounds"
        )
        excess = matching + last[c]
        push = forc32[pl.ds(c, blocks, stride=2), :] + excess
        source = TIME_STEP * PUSH_GAIN * push
        edge_low.append(gap[0] * source)
        edge_high.append(-gap[top_row] * source)
        x_top.append(jump[top_row, c] + gap[top_row] * excess)
    slip = slip_of(top_row, speed(x_top))
    share = 1.0 / (slip + edge[0])
    y_top = [
        (x_top[c] + edge_high[c] + edge[2 + c] + edge_low[c] * edge[1]) * share for c in range(2)
    ]
    x_top = [slip * y_top[c] for c in range(2)]

    def first_answer(m):
        if m == top_row:
            return x_top
        return [
            jump[m, c] + edge_low[c] * by_push[m] + y_top[c] * by_top[m] for c in range(2)
        ]

    def eliminate(m, ratio, state, ends, first):
        if first:
            x = first_answer(m)
            slip = slip_of(m, speed(x))
        else:
            x = [jump[m, c] for c in range(2)]
            slip = slip_of(m, held_r[m])
        if state is None:
            near = slip
            t = [x[c] + ends[c] for c in range(2)]
        else:
            above, h, t = state
            near = slip + above
            t = [x[c] + h * t[c] for c in range(2)]
        f = 1.0 / (near + 1.0)
        h = ratio * f
        return slip, near, f, t, (near * h, h, t)

    def forward(first):
        low, high = None, None
        for i in range(half):
            for m in (i, top_row - i):
                if m == i:
                    slip, near, f, t, low = eliminate(m, growth, low, edge_low, first)
                else:
                    slip, near, f, t, high = eliminate(m, decay, high, edge_high, first)
                held_f[m] = f
                held_s[m] = slip
                for c in range(2):
                    held_t[m, c] = t[c]
                if i == half - 1:
                    middle[m - i] = near

    def settle(m, y):
        slip = held_s[m]
        x = [slip * y[c] for c in range(2)]
        for c in range(2):
            jump[m, c] = x[c]
        held_r[m] = speed(x)

    def backward(final):
        f_high = held_f[half]
        share = 1.0 / (middle[0] + middle[1] * f_high)
        down, up = [], []
        for c in range(2):
            t_high = held_t[half, c]
            down.append((held_t[half - 1, c] + f_high * t_high) * share)
            up.append(f_high * (t_high + down[c]))
        if not final:
            settle(half - 1, down)
            settle(half, up)
        for i in range(half - 2, -1, -1):
            for m, y in ((i, down), (top_row - i, up)):
                if final and m != i:
                    continue
                f = held_f[m]
                for c in range(2):
                    y[c] = f * (held_t[m, c] + y[c])
                if not final:
                    settle(m, y)
        return down

    forward(True)

    def time_step(_, carry):
        backward(False)
        forward(False)
        return carry

    lax.fori_loop(2, STEPS, time_step, 0)
    down = backward(True)

    wall = [held_s[0] * down[c] for c in range(2)]
    wall_flux = (base[0] + quad[0] * speed(wall)) * (1.0 / TIME_STEP)
    lane = lax.broadcasted_iota(jnp.int32, live.shape, 1)
    own_live = jnp.sum(
        jnp.where(lane == me * grps + mine, live[...], 0).astype(F32), axis=1, keepdims=True
    )
    alive = lax.broadcasted_iota(jnp.int32, wide, 0).astype(F32) < own_live
    size = area[...]
    for c in range(2):
        shear = jnp.where(alive, wall_flux * wall[c], 0.0)
        shear_ref[pl.ds(c, blocks, stride=2), :] = shear
        piece = shear * size
        top = piece.astype(BF16).astype(F32)
        cells[pl.ds(c, blocks, stride=4), :] = top
        cells[pl.ds(2 + c, blocks, stride=4), :] = piece - top
    upper = lax.broadcasted_iota(jnp.int32, (8, faces), 0) < 4
    for p in range(blocks // 2):
        both = cells[pl.ds(8 * p, 8), :]
        pair = jnp.concatenate(
            [jnp.where(upper, both, 0.0), jnp.where(upper, 0.0, both)], axis=1
        ).astype(BF16)
        cells[pl.ds(8 * p, 8), :] = jnp.dot(pair, pick[p], preferred_element_type=F32)
    spots = lax.broadcasted_iota(jnp.int32, (rows // 2, faces), 0)
    sums = [jnp.zeros((rows // 2, faces), F32) for _ in range(2)]
    for b in range(blocks):
        here = spots == spot_at[b]
        for c in range(2):
            row = cells[pl.ds(4 * b + c, 1), :] + cells[pl.ds(4 * b + 2 + c, 1), :]
            sums[c] += jnp.where(here, jnp.broadcast_to(row, (rows // 2, faces)), 0.0)
    for c in range(2):
        early_out[pl.ds(c, rows // 2, stride=2), :] = sums[c]

    def force_copy(src, land, peer):
        return pltpu.make_async_remote_copy(
            src_ref=src,
            dst_ref=arrived.at[land],
            send_sem=force_send,
            recv_sem=force_recv,
            device_id={"dom": peer},
            device_id_type=MESH,
        )

    force_copy(early_out.at[pl.ds(0, rows)], lands[0], peers[0]).start()
    by_cell = cells[pl.ds(0, 4 * blocks), :]
    top = by_cell.astype(BF16)
    low = (by_cell - top.astype(F32)).astype(BF16)
    total = jnp.dot(
        place[...], jnp.concatenate([top, low], axis=0), preferred_element_type=F32
    )
    packed[...] = total.reshape(doms, rows, faces)
    for land, peer in zip(lands[1:], peers[1:]):
        force_copy(packed.at[peer], land, peer).start()
    forces = pltpu.make_async_remote_copy(
        src_ref=packed.at[pl.ds(0, doms - 1)],
        dst_ref=arrived,
        send_sem=force_send,
        recv_sem=force_recv,
        device_id={"dom": relay},
        device_id_type=MESH,
    )
    @pl.when(me == 0)
    def _():
        cells_of(1, cell_send, relay_recv).wait_send()

    @pl.when(me != 0)
    def _():
        cells_of(doms - 1, cell_send, cell_recv).wait_send()

    @pl.when(me == relay)
    def _():
        cells_of(doms - 2, relay_send, cell_recv).wait_send()

    forces.wait_send()
    forces.wait_recv()
    result = packed[me]
    for j in range(doms - 1):
        result += arrived[j]
    force_ref[...] = result


def emit(shear_ref, force_ref, shear_out, force_out):
    def run(sem):
        copies = (
            pltpu.make_async_copy(force_ref, force_out, sem.at[0]),
            pltpu.make_async_copy(shear_ref, shear_out, sem.at[1]),
        )
        for copy in copies:
            copy.start()
        for copy in copies:
            copy.wait()

    pl.run_scoped(run, pltpu.SemaphoreType.DMA((2,)))


def body(
    doms,
    grps,
    profile,
    forcing,
    height,
    area,
    stretch,
    face_cell,
    match_owner,
    match_block,
    live_blocks,
    cell_velocity,
):
    blocks, _, points, faces = profile.shape
    rows = 2 * cell_velocity.shape[0]
    everything = pl.BlockSpec(memory_space=pltpu.HBM)
    vmem = pl.BlockSpec(memory_space=pltpu.VMEM)
    deep = (points, blocks, faces)
    dma = pltpu.SemaphoreType.DMA
    vmem_bytes = 32 << 20
    args = (
        profile,
        forcing.reshape(2 * blocks, faces),
        height,
        area,
        stretch.reshape(1, blocks),
        face_cell,
        match_owner,
        match_block,
        live_blocks.reshape(1, -1),
        cell_velocity.reshape(rows, faces),
    )
    shear, force = pl.pallas_call(
        functools.partial(kernel, doms, grps),
        out_shape=(
            jax.ShapeDtypeStruct((2 * blocks, faces), F32),
            jax.ShapeDtypeStruct((rows, faces), F32),
        ),
        in_specs=[everything] * len(args),
        out_specs=(vmem, vmem),
        scratch_shapes=[pltpu.VMEM(arg.shape, arg.dtype) for arg in args[:-1]]
        + [
            pltpu.VMEM((doms, rows, faces), BF16),
            pltpu.VMEM((points, 2, blocks, faces), F32),
            pltpu.VMEM(deep, F32),
            pltpu.VMEM(deep, F32),
            pltpu.VMEM(deep, F32),
            pltpu.VMEM((points, 2, blocks, faces), F32),
            pltpu.VMEM(deep, F32),
            pltpu.VMEM(deep, F32),
            pltpu.VMEM(deep, F32),
            pltpu.VMEM(deep, F32),
            pltpu.VMEM(deep, F32),
            pltpu.VMEM(deep, F32),
            pltpu.VMEM((2, blocks, faces), F32),
            pltpu.VMEM((4, blocks, faces), F32),
            pltpu.VMEM((2, blocks, faces), F32),
            pltpu.VMEM((2, blocks, faces), F32),
            pltpu.VMEM((doms * rows + 8, faces), F32),
            pltpu.VMEM((2 * blocks + 8, faces), F32),
            pltpu.SMEM((1, blocks), jnp.int32),
            pltpu.SMEM((1, blocks), jnp.int32),
            pltpu.SMEM((blocks,), jnp.int32),
            pltpu.SMEM((blocks,), jnp.int32),
            pltpu.VMEM((rows + 16, faces), F32),
            pltpu.VMEM((blocks // 2, 2 * faces, faces), BF16),
            pltpu.VMEM((doms * rows, 8 * blocks), BF16),
            pltpu.VMEM((4 * blocks + 8, faces), F32),
            pltpu.VMEM((doms, rows, faces), F32),
            pltpu.VMEM((doms - 1, rows, faces), F32),
            pltpu.VMEM((2 * blocks, faces), F32),
            dma,
            dma,
            dma,
            dma,
            dma,
            dma,
        ],
        compiler_params=pltpu.CompilerParams(
            collective_id=0, has_side_effects=True, vmem_limit_bytes=vmem_bytes
        ),
        name="wall_model",
    )(*[pltpu.with_memory_space_constraint(x, pltpu.HBM) for x in args])
    shear, force = pl.pallas_call(
        emit,
        out_shape=(
            jax.ShapeDtypeStruct(shear.shape, F32),
            jax.ShapeDtypeStruct(force.shape, F32),
        ),
        in_specs=[pl.BlockSpec(memory_space=pl.ANY)] * 2,
        out_specs=(pl.BlockSpec(memory_space=pl.ANY),) * 2,
        compiler_params=pltpu.CompilerParams(vmem_limit_bytes=1 << 20),
        name="emit",
    )(shear, force)
    return (
        shear.reshape(blocks, 2, faces),
        force.reshape(cell_velocity.shape[0], 2, faces),
    )


def solution(mesh):
    in_specs = (
        P(("dom", "grp"), None, None, None),
        P(("dom", "grp"), None, None),
        P(("dom", "grp"), None),
        P(("dom", "grp"), None),
        P(("dom", "grp")),
        P(("dom", "grp"), None),
        P(None, "grp", None),
        P(None, "grp", None),
        P(),
        P(("dom", "grp"), None, None),
    )
    out_specs = (P(("dom", "grp"), None, None), P(("dom", "grp"), None, None))
    step = functools.partial(body, mesh.shape["dom"], mesh.shape["grp"])
    return jax.shard_map(step, mesh=mesh, in_specs=in_specs, out_specs=out_specs, check_vma=False)
```
